256 devices in a mesh: seq: 64 (over x, z, core), head: 4 (over y).
Axes of the slice: x: 4, y: 4, z: 8, core: 2. Of those that a mesh axis runs over, the one named last changes fastest.
Arguments:
- face_rows: bfloat16 [16384, 1024], P('seq', 'head'), may hold values from -400 to 400
- norm_gain: float32 [1024], replicated, may hold values from 0.25 to 1.75
- w_qkv: bfloat16 [1024, 3, 1024], P(None, None, 'head'), may hold values from -1.875 to 1.875
- w_out: bfloat16 [1024, 1024], P('head'), may hold values from -0.1875 to 0.1875
- segments: int32 [16384], P('seq'), may hold values from 0 to 3, never falling along the last dimension, each value on 1 to 8192 neighbouring positions
Outputs:
- mixed: bfloat16 [16384, 1024], P('seq', 'head')
The draws below stay inside these ranges and needn't reach their ends.
All inputs are finite; a program needn't handle non-finite values.
Results may differ from the reference program's by a relative error of at most 0.004.
The reference program's roundings to bfloat16 on the way count: a program that leaves them out, or rounds other values in their place, can miss the bound.
Values may be sent and summed in bfloat16 or wider, within the bound.
A program may use at most 128 MiB of HBM per device.

```python
import math
import jax
import jax.numpy as jnp
import numpy as np
from jax import lax

D = 1024
HEADS = 8
HD = 128
SEGS = 4
FACES = 16384


def draw_face_rows(key, part):
    key_noise = jax.random.fold_in(jax.random.fold_in(key, 11), 0)
    result = jnp.clip(jax.random.normal(key_noise, (FACES, D), jnp.float32), -4.0, 4.0)
    return result.astype(jnp.bfloat16)


def draw_w_qkv(key, part):
    key_noise = jax.random.fold_in(jax.random.fold_in(key, 23), 0)
    result = jnp.clip(jax.random.normal(key_noise, (D, 3, HEADS * HD), jnp.float32), -6.0, 6.0) * D ** (-0.5)
    return result.astype(jnp.bfloat16)


def level_of(own_key, dims, shards, least, largest):
    gain = 1.0
    for axis_at, parts in shards:
        draws = jax.random.uniform(jax.random.fold_in(jax.random.fold_in(own_key, 6), axis_at), (parts,), jnp.float32, least / len(shards), largest / len(shards))
        gain = gain * jnp.repeat(jnp.exp(draws), dims[axis_at] // parts).reshape((-1,) + (1,) * (len(dims) - 1 - axis_at))
    return gain


def profile(number_of, total, reach, lean):
    portions = [(1 << 20) // math.isqrt(standing ** lean) + 1 for standing in range(2, number_of + 1)]
    surplus, holding = total - reach - (number_of - 1), [1] * (number_of - 1)
    while surplus > 0:
        free = [i for i in range(number_of - 1) if holding[i] < reach]
        whole, remaining = sum([portions[i] for i in free]), surplus
        for i in free:
            extra = min(reach - holding[i], max(1, remaining * portions[i] // whole), surplus)
            holding[i] = holding[i] + extra
            surplus = surplus - extra
    return np.array([reach] + holding)


def ragged(own_key, amount, total, reach, slope):
    if amount == 2:
        one = jax.random.randint(own_key, (), max(1, total - reach), min(reach, total - 1) + 1)
        return jnp.stack([one, total - one])
    tallies = jnp.asarray(profile(amount, total, reach, slope), jnp.int32)
    twos = (amount - 1) // 2
    source_of, receiver = tallies[1:1 + 2 * twos:2], tallies[2:2 + 2 * twos:2]
    slack = jnp.minimum(source_of - 1, reach - receiver)
    passed = jax.random.randint(jax.random.fold_in(own_key, 1), (twos,), 0, 1 << 20) % (slack + 1)
    tallies = tallies.at[1:1 + 2 * twos:2].set(source_of - passed).at[2:2 + 2 * twos:2].set(receiver + passed)
    return tallies[jax.random.permutation(jax.random.fold_in(own_key, 2), amount)]


def normal_values(rng, extent, scale, limit, cuts=(), dtype=jnp.bfloat16):
    factor_of = level_of(rng, extent, cuts, -0.22, 0.18) if cuts else 1.0
    values = jax.random.normal(rng, extent, jnp.float32) * scale * factor_of
    return jnp.minimum(jnp.maximum(values, -limit), limit).astype(dtype)


def setup_inputs(seed: int = 0) -> dict:
    seeds = jax.random.split(jax.random.key(seed), 6)
    face_rows = draw_face_rows(jax.random.fold_in(seeds[5], 71), 0)
    norm_gain = jnp.clip(1.0 + 0.15 * jax.random.normal(seeds[1], (D,), jnp.float32), 0.25, 1.75)
    w_qkv = draw_w_qkv(jax.random.fold_in(seeds[5], 71), 0)
    w_out = normal_values(seeds[3], (HEADS * HD, D), (HEADS * HD) ** -0.5, 0.1875, ((0, 4),))
    segments = jnp.searchsorted(jnp.cumsum(ragged(seeds[4], SEGS, FACES, FACES // 2, 0)), jnp.arange(FACES), side="right").astype(jnp.int32)
    return {"face_rows": face_rows, "norm_gain": norm_gain, "w_qkv": w_qkv, "w_out": w_out, "segments": segments}


epsilon = 1e-05
masked_score = -1e+30

def reference(face_rows, norm_gain, w_qkv, w_out, segments):
    width = HEADS * HD
    values32 = face_rows.astype(jnp.float32)
    normed = (values32 * lax.rsqrt(lax.optimization_barrier(jnp.mean(values32 * values32, axis=1, keepdims=True)) + epsilon) * norm_gain).astype(jnp.bfloat16)
    projected = jnp.dot(normed, w_qkv.reshape(D, 3 * width), preferred_element_type=jnp.float32)
    queries = (projected[:, :width] * (1.0 / math.sqrt(HD))).astype(jnp.bfloat16).reshape(FACES, HEADS, HD)
    key_rows = projected[:, width:2 * width].astype(jnp.bfloat16).reshape(FACES, HEADS, HD)
    value_rows = projected[:, 2 * width:].astype(jnp.bfloat16).reshape(FACES, HEADS, HD)
    positions = lax.iota(jnp.int32, FACES)
    block = math.gcd(FACES, 256)
    pieces = []
    for first_row in range(0, FACES, block):
        last_row = first_row + block
        query_block = queries[first_row:last_row].astype(jnp.float32)
        key_block = key_rows[:last_row].astype(jnp.float32)
        value_block = value_rows[:last_row].astype(jnp.float32)
        scores = jnp.einsum('qhd,khd->hqk', query_block, key_block)
        allowed = (positions[None, :last_row] <= positions[first_row:last_row, None]) & (segments[None, :last_row] == segments[first_row:last_row, None])
        scores = jnp.where(allowed[None], scores, masked_score)
        row_max = lax.optimization_barrier(jnp.max(scores, axis=2, keepdims=True))
        weights = jnp.where(allowed[None], jnp.exp(scores - row_max), 0.0)
        totals = lax.optimization_barrier(jnp.sum(weights, axis=2, keepdims=True))
        rounded = weights.astype(jnp.bfloat16).astype(jnp.float32)
        result = jnp.einsum('hqk,khd->hqd', rounded, value_block) / totals
        pieces.append(jnp.transpose(result, (1, 0, 2)).reshape(block, width).astype(jnp.bfloat16))
    attended = jnp.concatenate(pieces, axis=0)
    return jnp.dot(attended, w_out, preferred_element_type=jnp.float32).astype(jnp.bfloat16)
```

```python
import functools
import math

import jax
import jax.numpy as jnp
from jax import lax
from jax.experimental import pallas as pl
from jax.experimental.pallas import tpu as pltpu
from jax.sharding import PartitionSpec as P

MESH = pl.DeviceIdType.MESH
HD = 128
epsilon = 1e-05
masked_score = -1e30
PLAN = (
    (870258657, 812574466, 850160585, 871119793, 829180757, 541631245, 7),
    (882874144, 870062881, 887908237, 896281557, 824998833, 533274, 5),
    (1021257508, 839658277, 820774869, 829180829, 900496153, 785, 5),
    (958347176, 815545124, 839685973, 829384530, 837711706, 769, 5),
    (895436588, 1033653160, 849173284, 806319877, 871118618, 833, 5),
    (1033852720, 866999212, 940390237, 907842344, 811345681, 798, 5),
    (1037952948, 873224112, 891091756, 848107290, 807179017, 781, 5),
    (937190208, 827123457, 857621317, 952957769, 828154733, 804, 4),
    (613287492, 1012665149, 815536926, 828323769, 854354698, 829180817, 7),
    (1012826696, 840702921, 883767229, 1000143633, 896297877, 801554, 7),
    (1021257636, 839730954, 854546213, 829224737, 832338770, 794, 7),
    (1025324968, 1029449508, 839732005, 820930358, 970812161, 798, 5),
    (895469484, 819743656, 849307396, 836528901, 837606272, 769, 5),
    (1033721648, 867087121, 819733469, 944601984, 811345697, 790, 5),
    (990734260, 873428757, 824095684, 811475742, 815544090, 769, 5),
    (1071539136, 807211838, 1015867284, 811483957, 857487113, 780, 4),
)
EVENTS = 3 * len(PLAN[0])
ROWS = 256
BLOCK = 512
INFO = 16
SLOT = 2 * BLOCK + 2 * INFO


def pick(values, index):
    result = jnp.int32(values[0])
    for at in range(1, len(values)):
        result = jnp.where(index == at, jnp.int32(values[at]), result)
    return result


def kernel(
    x_hbm, gain_ref, wqkv_hbm, wout_hbm, seg_ref, out_ref,
    xbuf, wqkv, wcol, kv, give, qrows, qmask, acc, run_max, run_sum, ogive, att,
    local_sem, x_send, x_recv, w_send, w_recv, s_send, s_recv, kv_send, kv_recv, o_send, o_recv,
):
    f32, bf16 = jnp.float32, jnp.bfloat16
    seq, head = lax.axis_index("seq"), lax.axis_index("head")
    core = lax.rem(seq, 2)
    chip = lax.div(seq, 2)
    z = lax.rem(chip, 8)
    x = lax.div(chip, 8)
    other = 1 - core

    def at(xx, zz, cc):
        return (xx * 8 + zz) * 2 + cc

    z_up, z_down = lax.rem(z + 1, 8), lax.rem(z + 7, 8)
    x_up, x_down = lax.rem(x + 1, 4), lax.rem(x + 3, 4)
    up = (at(x, z_up, core), head)
    down = (at(x, z_down, core), head)
    right = (at(x_up, z, core), head)
    left = (at(x_down, z, core), head)
    partner = (at(x, z, other), head)
    y_of = [lax.rem(head + j, 4) for j in range(4)]

    barrier = pltpu.get_barrier_semaphore()
    greeted = [up, down, right, left, partner]
    for j in range(1, 4):
        greeted.append((seq, y_of[j]))
        greeted.append((at(x, z, other), y_of[j]))
    for device in greeted:
        pl.semaphore_signal(barrier, inc=1, device_id=device, device_id_type=MESH)

    mine = pltpu.make_async_copy(x_hbm, xbuf.at[head], local_sem.at[0])
    mine.start()
    weights_in = pltpu.make_async_copy(wqkv_hbm, wqkv, local_sem.at[1])
    weights_in.start()
    columns = pl.ds(pl.multiple_of(head * ROWS, ROWS), ROWS)
    wcol_in = pltpu.make_async_copy(wout_hbm.at[:, columns], wcol.at[head], local_sem.at[2])
    wcol_in.start()

    seg = seg_ref[...]
    lane = lax.broadcasted_iota(jnp.int32, (1, HD), 1)
    sub = lax.broadcasted_iota(jnp.int32, (INFO, HD), 0)
    lower = jnp.zeros((1, HD), f32)
    upper = jnp.zeros((1, HD), f32)
    for t in range(1, 5):
        before = jnp.sum(jnp.where(seg < t, 1.0, 0.0).astype(f32), axis=1, keepdims=True)
        before = before[0:1] + before[1:2]
        lower = jnp.where(lane == t, before, lower)
        upper = jnp.where(lane == t - 1, before, upper)
    lower = jnp.where(lane < 4, lower, 0.0)
    info = jnp.where(sub == 0, lower, jnp.where(sub == 1, upper, 0.0)).astype(bf16)

    pl.semaphore_wait(barrier, len(greeted))

    x_copies = []
    for j in range(1, 4):
        copy = pltpu.make_async_remote_copy(
            src_ref=x_hbm, dst_ref=xbuf.at[head], send_sem=x_send.at[j], recv_sem=x_recv.at[head],
            device_id=(seq, y_of[j]), device_id_type=MESH)
        copy.start()
        x_copies.append(copy)
    mine.wait()
    weights_in.wait()
    wcol_in.wait()
    for j in range(1, 4):
        pltpu.make_async_remote_copy(
            src_ref=x_hbm, dst_ref=xbuf.at[y_of[j]], send_sem=x_send.at[j], recv_sem=x_recv.at[y_of[j]],
            device_id=(seq, y_of[j]), device_id_type=MESH).wait_recv()

    w_copies = []
    for j in range(1, 4):
        theirs = pl.ds(pl.multiple_of(y_of[j] * ROWS, ROWS), ROWS)
        copy = pltpu.make_async_remote_copy(
            src_ref=wout_hbm.at[:, theirs], dst_ref=wcol.at[head], send_sem=w_send.at[j],
            recv_sem=w_recv.at[head], device_id=(seq, y_of[j]), device_id_type=MESH)
        copy.start()
        w_copies.append(copy)

    squares = jnp.zeros((ROWS, 1), f32)
    for y in range(4):
        part = xbuf[y].astype(f32)
        squares = squares + jnp.sum(part * part, axis=1, keepdims=True)
    scale = lax.rsqrt(squares * (1.0 / 1024.0) + epsilon)
    normed = []
    for y in range(4):
        gain = gain_ref[:, y * ROWS : (y + 1) * ROWS]
        normed.append((xbuf[y].astype(f32) * scale * gain).astype(bf16))

    def project(which):
        total = None
        for y in range(4):
            term = jnp.dot(
                normed[y], wqkv[which, y * ROWS : (y + 1) * ROWS, :], preferred_element_type=f32)
            total = term if total is None else total + term
        return total

    own = pl.ds(pl.multiple_of(core * ROWS, ROWS), ROWS)
    own_values = pl.ds(pl.multiple_of(BLOCK + core * ROWS, ROWS), ROWS)
    own_info = pl.ds(pl.multiple_of(2 * BLOCK + core * INFO, INFO), INFO)

    def swap(j, source, target):
        return pltpu.make_async_remote_copy(
            src_ref=source, dst_ref=target, send_sem=s_send.at[j], recv_sem=s_recv.at[j],
            device_id=partner, device_id_type=MESH)

    s_copies = []
    give[3, 0:INFO, :] = info
    kv[chip, own_info, :] = info
    for j, target in ((1, kv.at[chip, own]), (2, kv.at[chip, own_values]), (0, qrows.at[own])):
        columns_of = project(j)
        if j == 0:
            columns_of = columns_of * (1.0 / math.sqrt(HD))
        columns_of = columns_of.astype(bf16)
        first, second = columns_of[:, :HD], columns_of[:, HD:]
        give[j] = jnp.where(core == 0, second, first)
        copy = swap(j, give.at[j], target)
        copy.start()
        s_copies.append(copy)
        if j == 1:
            copy = swap(3, give.at[3, 0:INFO], kv.at[chip, own_info])
            copy.start()
            s_copies.append(copy)
        target[...] = jnp.where(core == 0, first, second)
    for copy in s_copies:
        copy.wait_recv()

    mine_at = core * 8 + z
    words = [pick([row[i] for row in PLAN], mine_at) for i in range(len(PLAN[0]))]

    def event(e):
        third = lax.div(e, 3)
        word = words[0]
        for i in range(1, len(words)):
            word = jnp.where(third == i, words[i], word)
        place = lax.rem(e, 3)
        word = jnp.where(place == 0, word, jnp.where(place == 1, lax.div(word, 1024), lax.div(word, 1024 * 1024)))
        code = lax.rem(word, 1024)
        back = lax.rem(code, 4)
        source_z = lax.rem(lax.div(code, 4), 8)
        flag = [lax.rem(lax.div(code, 32 << i), 2) == 1 for i in range(5)]
        column = x - back
        valid = flag[4] & (column >= 0)
        slot = jnp.where(column >= 0, column, 0) * 8 + source_z
        return valid, slot, flag

    def hand_on(direction, slot):
        device = (up, down, right)[direction]
        return pltpu.make_async_remote_copy(
            src_ref=kv.at[slot], dst_ref=kv.at[slot], send_sem=kv_send.at[direction, slot],
            recv_sem=kv_recv.at[slot], device_id=device, device_id_type=MESH)

    def ways(flag):
        return (flag[0], flag[1], flag[2] & (x < 3))

    own_words = [pick([row[-1] for row in PLAN], mine_at)]
    own_flag = [lax.rem(lax.div(own_words[0], 1 << i), 2) == 1 for i in range(3)]
    for direction, go in enumerate(ways(own_flag)):
        @pl.when(go)
        def _(direction=direction):
            hand_on(direction, chip).start()

    row = lax.broadcasted_iota(jnp.int32, (ROWS, HD), 0).astype(f32)
    lanes = lax.broadcasted_iota(jnp.int32, (ROWS, HD), 1)

    def inside(slot, half):
        bounds = kv[slot, 2 * BLOCK + half * INFO : 2 * BLOCK + (half + 1) * INFO, :].astype(f32)
        return (row >= bounds[0:1, :]) & (row < bounds[1:2, :])

    for half in range(2):
        qmask[half * ROWS : (half + 1) * ROWS, :] = jnp.where(
            inside(chip, half) | (lanes >= 4), 0.0, masked_score).astype(bf16)

    def attend(slot, first):
        key_mask = jnp.concatenate(
            [jnp.where(inside(slot, half), 1.0, 0.0).astype(bf16) for half in range(2)], axis=0)
        keys = jnp.concatenate([kv[slot, 0:BLOCK, :], key_mask], axis=1)
        values = kv[slot, BLOCK : 2 * BLOCK, :]
        for part in range(2):
            rows = slice(part * ROWS, (part + 1) * ROWS)
            queries = jnp.concatenate([qrows[rows, :], qmask[rows, :]], axis=1)
            scores = lax.dot_general(
                queries, keys, (((1,), (1,)), ((), ())), preferred_element_type=f32)
            if first:
                q_at = lax.broadcasted_iota(jnp.int32, (ROWS, BLOCK), 0) + part * ROWS
                k_at = lax.broadcasted_iota(jnp.int32, (ROWS, BLOCK), 1)
                scores = jnp.where(k_at <= q_at, scores, masked_score)
                new_max = jnp.max(scores, axis=1, keepdims=True)
            else:
                old_max = run_max[rows, 0:1]
                new_max = jnp.maximum(old_max, jnp.max(scores, axis=1, keepdims=True))
            weights = jnp.exp(scores - new_max)
            total = jnp.sum(weights, axis=1, keepdims=True)
            product = jnp.dot(weights.astype(bf16), values, preferred_element_type=f32)
            if not first:
                factor = jnp.exp(old_max - new_max)
                total = total + run_sum[rows, 0:1] * factor
                product = product + acc[rows, :] * factor
            run_max[rows, :] = jnp.broadcast_to(new_max, (ROWS, HD))
            run_sum[rows, :] = jnp.broadcast_to(total, (ROWS, HD))
            acc[rows, :] = product

    attend(chip, True)

    def step(e, carry):
        valid, slot, flag = event(e)

        @pl.when(valid)
        def _():
            hand_on(0, slot).wait_recv()
            for direction, go in enumerate(ways(flag)):
                @pl.when(go)
                def _(direction=direction):
                    hand_on(direction, slot).start()

            @pl.when(flag[3])
            def _():
                attend(slot, False)

        return carry

    lax.fori_loop(0, EVENTS - 3, step, 0)

    for half in range(2):
        rows = slice(half * ROWS, (half + 1) * ROWS)
        ogive[half] = (acc[rows, :] / run_sum[rows, 0:1]).astype(bf16)

    o_copies = []
    lot = head * 2 + core
    for j in range(4):
        for c in range(2):
            if j == 0 and c == 0:
                continue
            row_core = core if c == 0 else other
            copy = pltpu.make_async_remote_copy(
                src_ref=ogive.at[row_core], dst_ref=att.at[lot], send_sem=o_send.at[j * 2 + c],
                recv_sem=o_recv.at[lot], device_id=(at(x, z, row_core), y_of[j]), device_id_type=MESH)
            copy.start()
            o_copies.append(copy)
    att[lot] = ogive[core]

    for j in range(1, 4):
        pltpu.make_async_remote_copy(
            src_ref=wout_hbm.at[:, columns], dst_ref=wcol.at[y_of[j]], send_sem=w_send.at[j],
            recv_sem=w_recv.at[y_of[j]], device_id=(seq, y_of[j]), device_id_type=MESH).wait_recv()
    for j in range(4):
        for c in range(2):
            if j == 0 and c == 0:
                continue
            lot_of = y_of[j] * 2 + (core if c == 0 else other)
            pltpu.make_async_remote_copy(
                src_ref=ogive.at[core], dst_ref=att.at[lot_of], send_sem=o_send.at[j * 2 + c],
                recv_sem=o_recv.at[lot_of], device_id=partner, device_id_type=MESH).wait_recv()

    total = None
    for y in range(4):
        both = jnp.concatenate([att[2 * y], att[2 * y + 1]], axis=1)
        term = jnp.dot(both, wcol[y], preferred_element_type=f32)
        total = term if total is None else total + term
    out_ref[...] = total.astype(bf16)

    for copy in x_copies + w_copies + s_copies + o_copies:
        copy.wait_send()
    for direction, go in enumerate(ways(own_flag)):
        @pl.when(go)
        def _(direction=direction):
            hand_on(direction, chip).wait_send()

    def drain(e, carry):
        valid, slot, flag = event(e)
        for direction, go in enumerate(ways(flag)):
            @pl.when(valid & go)
            def _(direction=direction):
                hand_on(direction, slot).wait_send()
        return carry

    lax.fori_loop(0, EVENTS - 3, drain, 0)


def per_device(face_rows, norm_gain, w_qkv, w_out, segments):
    bf16, f32 = jnp.bfloat16, jnp.float32
    vmem = pl.BlockSpec(memory_space=pltpu.VMEM)
    hbm = pl.BlockSpec(memory_space=pl.ANY)
    dma = pltpu.SemaphoreType.DMA
    return pl.pallas_call(
        kernel,
        name="face_attention",
        out_shape=jax.ShapeDtypeStruct((ROWS, ROWS), bf16),
        in_specs=[hbm, vmem, hbm, hbm, vmem],
        out_specs=vmem,
        scratch_shapes=[
            pltpu.VMEM((4, ROWS, ROWS), bf16),
            pltpu.VMEM((3, 1024, ROWS), bf16),
            pltpu.VMEM((4, ROWS, ROWS), bf16),
            pltpu.VMEM((32, SLOT, HD), bf16),
            pltpu.VMEM((4, ROWS, HD), bf16),
            pltpu.VMEM((BLOCK, HD), bf16),
            pltpu.VMEM((BLOCK, HD), bf16),
            pltpu.VMEM((BLOCK, HD), f32),
            pltpu.VMEM((BLOCK, HD), f32),
            pltpu.VMEM((BLOCK, HD), f32),
            pltpu.VMEM((2, ROWS, HD), bf16),
            pltpu.VMEM((8, ROWS, HD), bf16),
            dma((3,)),
            dma((4,)), dma((4,)),
            dma((4,)), dma((4,)),
            dma((4,)), dma((4,)),
            dma((3, 32)), dma((32,)),
            dma((8,)), dma((8,)),
        ],
        compiler_params=pltpu.CompilerParams(
            collective_id=0, has_side_effects=True, vmem_limit_bytes=48 * 2**20),
    )(
        face_rows,
        norm_gain.reshape(1, 1024),
        jnp.transpose(w_qkv, (1, 0, 2)),
        w_out,
        segments.reshape(2, HD),
    )


def solution(mesh):
    in_specs = (P("seq", "head"), P(), P(None, None, "head"), P("head", None), P("seq"))
    out_specs = P("seq", "head")
    return jax.shard_map(
        per_device, mesh=mesh, in_specs=in_specs, out_specs=out_specs, check_vma=False
    )
```

```python
import functools
import math

import jax
import jax.numpy as jnp
from jax import lax
from jax.experimental import pallas as pl
from jax.experimental.pallas import tpu as pltpu
from jax.sharding import PartitionSpec as P

MESH = pl.DeviceIdType.MESH
HD = 128
epsilon = 1e-05
masked_score = -1e30
PLAN = (
    (198721, 0, 0, 0, 0, 0, 7),
    (557122, 0, 0, 0, 0, 0, 7),
    (557601, 0, 0, 0, 0, 0, 7),
    (705332898, 0, 0, 0, 0, 0, 5),
    (707300485, 524801, 0, 0, 0, 0, 5),
    (671780516, 525826, 0, 0, 0, 0, 7),
    (604541605, 673877569, 0, 0, 0, 0, 5),
    (739777088, 541657733, 643, 0, 0, 0, 4),
    (772316233, 711591114, 710414018, 644, 0, 0, 7),
    (579503178, 571083431, 676860611, 550, 0, 0, 7),
    (607849001, 544776705, 542839296, 518, 0, 0, 7),
    (714779331, 572136132, 713627138, 524935, 0, 0, 5),
    (608742541, 609950378, 546867911, 537429507, 520, 0, 5),
    (575280812, 612019910, 546843272, 539591235, 513, 0, 7),
    (746239718, 542712364, 538481225, 540682923, 526848, 0, 5),
    (552149735, 639146697, 576337408, 575156810, 539496075, 0, 4),
    (780713041, 719987922, 548931274, 537434797, 540684802, 541597189, 7),
    (587899986, 579480239, 607690443, 538456578, 543734413, 529924, 7),
    (616245809, 587729417, 545787407, 544749260, 543692356, 526, 7),
    (723176139, 686502467, 618146345, 609927716, 545856143, 519, 5),
    (617139349, 618347186, 581647941, 548936209, 578294313, 541192, 5),
    (583677620, 620416718, 688396869, 616056338, 546843240, 519, 7),
    (754636526, 621335046, 622343687, 725100076, 545795730, 522, 5),
    (578372335, 585844246, 693641833, 558451245, 549080620, 522, 4),
    (654892121, 594035802, 557327954, 545831477, 548950538, 549993997, 3),
    (596165722, 587745847, 616087123, 546853386, 552131093, 538124, 3),
    (624511545, 596126225, 554184215, 553145940, 552089164, 534, 3),
    (597224019, 560550475, 626543153, 618193452, 554252823, 527, 1),
    (598299195, 618223190, 563661399, 588795406, 554221068, 536, 1),
    (591943228, 628682326, 562575949, 624453146, 555240048, 527, 1),
    (628684406, 629731854, 630740495, 599279156, 554192410, 530, 1),
    (586769015, 594109982, 567820913, 566848053, 557346356, 530, 0),
    (135, 0, 0, 0, 0, 0, 7),
    (672, 0, 0, 0, 0, 0, 5),
    (688673, 0, 0, 0, 0, 0, 5),
    (571115170, 0, 0, 0, 0, 0, 5),
    (706382499, 672, 0, 0, 0, 0, 5),
    (707431972, 524961, 0, 0, 0, 0, 5),
    (709362213, 574261383, 673, 0, 0, 0, 5),
    (676993600, 540674692, 513, 0, 0, 0, 3),
    (739836047, 539663079, 541658629, 0, 0, 0, 7),
    (740886184, 711594563, 542769703, 0, 0, 0, 5),
    (713598658, 571151043, 538614469, 551, 0, 0, 5),
    (608767658, 579409577, 537462274, 531974, 0, 0, 5),
    (744140356, 714608298, 713693698, 537396743, 0, 0, 5),
    (716747333, 574167722, 537599657, 545785346, 516, 0, 5),
    (717759021, 612046991, 582658624, 714674693, 538446339, 0, 5),
    (577387080, 538588736, 682242789, 548966919, 539502083, 0, 3),
    (748232855, 572177135, 551132682, 543692363, 541592067, 524812, 7),
    (749282992, 684264011, 538492590, 578429507, 67703309, 529926, 5),
    (539543242, 751513264, 575245864, 547011277, 578338373, 518, 5),
    (617164466, 587806385, 545859082, 552078853, 553130532, 519, 5),
    (752537164, 643313330, 686303921, 553196208, 544743945, 516, 5),
    (725144141, 582564530, 754632197, 546843144, 645405200, 524, 5),
    (726155829, 620443799, 591055432, 617159181, 547892913, 531977, 5),
    (585783888, 546985544, 39473901, 583548562, 555232787, 535047, 3),
    (662259280, 556312118, 624449135, 548944397, 558379530, 520, 3),
    (623461944, 558443091, 546889270, 586695243, 76100117, 538126, 1),
    (547939922, 625561144, 583642672, 555276885, 586735181, 526, 1),
    (625561146, 596203065, 554255890, 560475661, 561527340, 527, 1),
    (626585172, 651710010, 560482873, 561592888, 553140753, 524, 1),
    (599323221, 590961210, 628680205, 555239952, 653802008, 532, 1),
    (600334909, 621370966, 559476282, 597250638, 555239955, 527, 1),
    (594049624, 555251280, 47739509, 591945242, 563629595, 543247, 0),
)
EVENTS = 3 * (len(PLAN[0]) - 1)
ROWS = 256
BLOCK = 512
INFO = 16
SLOT = 2 * BLOCK + 2 * INFO


def pick(values, index):
    result = jnp.int32(values[0])
    for at in range(1, len(values)):
        result = jnp.where(index == at, jnp.int32(values[at]), result)
    return result


def kernel(
    x_hbm, gain_ref, wqkv_hbm, wout_hbm, seg_ref, out_ref,
    xbuf, wqkv, wcol, kv, give, qrows, qmask, acc, run_max, run_sum, ogive, att,
    local_sem, x_send, x_recv, w_send, w_recv, s_send, s_recv, kv_send, kv_recv, o_send, o_recv,
):
    f32, bf16 = jnp.float32, jnp.bfloat16
    seq, head = lax.axis_index("seq"), lax.axis_index("head")
    core = lax.rem(seq, 2)
    chip = lax.div(seq, 2)
    z = lax.rem(chip, 8)
    x = lax.div(chip, 8)
    other = 1 - core

    def at(xx, zz, cc):
        return (xx * 8 + zz) * 2 + cc

    z_up, z_down = lax.rem(z + 1, 8), lax.rem(z + 7, 8)
    x_up, x_down = lax.rem(x + 1, 4), lax.rem(x + 3, 4)
    up = (at(x, z_up, core), head)
    down = (at(x, z_down, core), head)
    right = (at(x_up, z, core), head)
    left = (at(x_down, z, core), head)
    partner = (at(x, z, other), head)
    y_of = [lax.rem(head + j, 4) for j in range(4)]

    barrier = pltpu.get_barrier_semaphore()
    greeted = [up, down, right, left, partner]
    for j in range(1, 4):
        greeted.append((seq, y_of[j]))
        greeted.append((at(x, z, other), y_of[j]))
    for device in greeted:
        pl.semaphore_signal(barrier, inc=1, device_id=device, device_id_type=MESH)

    mine = pltpu.make_async_copy(x_hbm, xbuf.at[head], local_sem.at[0])
    mine.start()
    weights_in = pltpu.make_async_copy(wqkv_hbm, wqkv, local_sem.at[1])
    weights_in.start()
    columns = pl.ds(pl.multiple_of(head * ROWS, ROWS), ROWS)
    wcol_in = pltpu.make_async_copy(wout_hbm.at[:, columns], wcol.at[head], local_sem.at[2])
    wcol_in.start()

    seg = seg_ref[...]
    lane = lax.broadcasted_iota(jnp.int32, (1, HD), 1)
    sub = lax.broadcasted_iota(jnp.int32, (INFO, HD), 0)
    lower = jnp.zeros((1, HD), f32)
    upper = jnp.zeros((1, HD), f32)
    for t in range(1, 5):
        before = jnp.sum(jnp.where(seg < t, 1.0, 0.0).astype(f32), axis=1, keepdims=True)
        before = before[0:1] + before[1:2]
        lower = jnp.where(lane == t, before, lower)
        upper = jnp.where(lane == t - 1, before, upper)
    lower = jnp.where(lane < 4, lower, 0.0)
    info = jnp.where(sub == 0, lower, jnp.where(sub == 1, upper, 0.0)).astype(bf16)

    mine_at = core * 32 + chip
    words = [pick([row[i] for row in PLAN], mine_at) for i in range(len(PLAN[0]))]
    pl.semaphore_wait(barrier, len(greeted))

    x_copies = []
    for j in range(1, 4):
        copy = pltpu.make_async_remote_copy(
            src_ref=x_hbm, dst_ref=xbuf.at[head], send_sem=x_send.at[j], recv_sem=x_recv.at[head],
            device_id=(seq, y_of[j]), device_id_type=MESH)
        copy.start()
        x_copies.append(copy)
    mine.wait()
    weights_in.wait()
    wcol_in.wait()
    for j in range(1, 4):
        pltpu.make_async_remote_copy(
            src_ref=x_hbm, dst_ref=xbuf.at[y_of[j]], send_sem=x_send.at[j], recv_sem=x_recv.at[y_of[j]],
            device_id=(seq, y_of[j]), device_id_type=MESH).wait_recv()

    w_copies = []
    for j in range(1, 4):
        theirs = pl.ds(pl.multiple_of(y_of[j] * ROWS, ROWS), ROWS)
        copy = pltpu.make_async_remote_copy(
            src_ref=wout_hbm.at[:, theirs], dst_ref=wcol.at[head], send_sem=w_send.at[j],
            recv_sem=w_recv.at[head], device_id=(seq, y_of[j]), device_id_type=MESH)
        copy.start()
        w_copies.append(copy)

    squares = jnp.zeros((ROWS, 1), f32)
    for y in range(4):
        part = xbuf[y].astype(f32)
        squares = squares + jnp.sum(part * part, axis=1, keepdims=True)
    scale = lax.rsqrt(squares * (1.0 / 1024.0) + epsilon)
    normed = []
    for y in range(4):
        gain = gain_ref[:, y * ROWS : (y + 1) * ROWS]
        normed.append((xbuf[y].astype(f32) * scale * gain).astype(bf16))

    def project(which):
        total = None
        for y in range(4):
            term = jnp.dot(
                normed[y], wqkv[which, y * ROWS : (y + 1) * ROWS, :], preferred_element_type=f32)
            total = term if total is None else total + term
        return total

    own = pl.ds(pl.multiple_of(core * ROWS, ROWS), ROWS)
    own_values = pl.ds(pl.multiple_of(BLOCK + core * ROWS, ROWS), ROWS)
    own_info = pl.ds(pl.multiple_of(2 * BLOCK + core * INFO, INFO), INFO)

    def swap(j, source, target):
        return pltpu.make_async_remote_copy(
            src_ref=source, dst_ref=target, send_sem=s_send.at[j], recv_sem=s_recv.at[j],
            device_id=partner, device_id_type=MESH)

    s_copies = []
    give[3, 0:INFO, :] = info
    kv[chip, own_info, :] = info
    for j, target in ((1, kv.at[chip, own]), (2, kv.at[chip, own_values]), (0, qrows.at[own])):
        columns_of = project(j)
        if j == 0:
            columns_of = columns_of * (1.0 / math.sqrt(HD))
        columns_of = columns_of.astype(bf16)
        first, second = columns_of[:, :HD], columns_of[:, HD:]
        give[j] = jnp.where(core == 0, second, first)
        copy = swap(j, give.at[j], target)
        copy.start()
        s_copies.append(copy)
        if j == 1:
            copy = swap(3, give.at[3, 0:INFO], kv.at[chip, own_info])
            copy.start()
            s_copies.append(copy)
        target[...] = jnp.where(core == 0, first, second)
    for copy in s_copies:
        copy.wait_recv()

    def event(e):
        third = lax.div(e, 3)
        word = words[0]
        for i in range(1, len(words) - 1):
            word = jnp.where(third == i, words[i], word)
        place = lax.rem(e, 3)
        word = jnp.where(place == 0, word, jnp.where(place == 1, lax.div(word, 1024), lax.div(word, 1024 * 1024)))
        code = lax.rem(word, 1024)
        slot = lax.rem(code, 32)
        flag = [lax.rem(lax.div(code, 32 << i), 2) == 1 for i in range(5)]
        return code >= 32, slot, flag

    def hand_on(direction, slot):
        device = (up, down, right, left)[direction]
        return pltpu.make_async_remote_copy(
            src_ref=kv.at[slot], dst_ref=kv.at[slot], send_sem=kv_send.at[direction, slot],
            recv_sem=kv_recv.at[slot], device_id=device, device_id_type=MESH)

    own_flag = [lax.rem(lax.div(words[-1], 1 << i), 2) == 1 for i in range(4)]
    for direction in range(4):
        @pl.when(own_flag[direction])
        def _(direction=direction):
            hand_on(direction, chip).start()

    row = lax.broadcasted_iota(jnp.int32, (ROWS, HD), 0).astype(f32)
    lanes = lax.broadcasted_iota(jnp.int32, (ROWS, HD), 1)

    def inside(slot, half):
        bounds = kv[slot, 2 * BLOCK + half * INFO : 2 * BLOCK + (half + 1) * INFO, :].astype(f32)
        return (row >= bounds[0:1, :]) & (row < bounds[1:2, :])

    for half in range(2):
        qmask[half * ROWS : (half + 1) * ROWS, :] = jnp.where(
            inside(chip, half) | (lanes >= 4), 0.0, masked_score).astype(bf16)

    def attend(slot, first):
        key_mask = jnp.concatenate(
            [jnp.where(inside(slot, half), 1.0, 0.0).astype(bf16) for half in range(2)], axis=0)
        keys = jnp.concatenate([kv[slot, 0:BLOCK, :], key_mask], axis=1)
        values = kv[slot, BLOCK : 2 * BLOCK, :]
        for part in range(2):
            rows = slice(part * ROWS, (part + 1) * ROWS)
            queries = jnp.concatenate([qrows[rows, :], qmask[rows, :]], axis=1)
            scores = lax.dot_general(
                queries, keys, (((1,), (1,)), ((), ())), preferred_element_type=f32)
            if first:
                q_at = lax.broadcasted_iota(jnp.int32, (ROWS, BLOCK), 0) + part * ROWS
                k_at = lax.broadcasted_iota(jnp.int32, (ROWS, BLOCK), 1)
                scores = jnp.where(k_at <= q_at, scores, masked_score)
                new_max = jnp.max(scores, axis=1, keepdims=True)
            else:
                old_max = run_max[rows, 0:1]
                new_max = jnp.maximum(old_max, jnp.max(scores, axis=1, keepdims=True))
            weights = jnp.exp(scores - new_max)
            total = jnp.sum(weights, axis=1, keepdims=True)
            product = jnp.dot(weights.astype(bf16), values, preferred_element_type=f32)
            if not first:
                factor = jnp.exp(old_max - new_max)
                total = total + run_sum[rows, 0:1] * factor
                product = product + acc[rows, :] * factor
            run_max[rows, :] = jnp.broadcast_to(new_max, (ROWS, HD))
            run_sum[rows, :] = jnp.broadcast_to(total, (ROWS, HD))
            acc[rows, :] = product

    attend(chip, True)

    def step(e, carry):
        valid, slot, flag = event(e)

        @pl.when(valid)
        def _():
            hand_on(0, slot).wait_recv()
            for direction in range(4):
                @pl.when(flag[direction])
                def _(direction=direction):
                    hand_on(direction, slot).start()

            @pl.when(flag[4])
            def _():
                attend(slot, False)

        return carry

    lax.fori_loop(0, EVENTS, step, 0)

    for half in range(2):
        rows = slice(half * ROWS, (half + 1) * ROWS)
        ogive[half] = (acc[rows, :] / run_sum[rows, 0:1]).astype(bf16)

    o_copies = []
    lot = head * 2 + core
    for j in range(4):
        for c in range(2):
            if j == 0 and c == 0:
                continue
            row_core = core if c == 0 else other
            copy = pltpu.make_async_remote_copy(
                src_ref=ogive.at[row_core], dst_ref=att.at[lot], send_sem=o_send.at[j * 2 + c],
                recv_sem=o_recv.at[lot], device_id=(at(x, z, row_core), y_of[j]), device_id_type=MESH)
            copy.start()
            o_copies.append(copy)
    att[lot] = ogive[core]

    for direction in range(4):
        @pl.when(own_flag[direction])
        def _(direction=direction):
            hand_on(direction, chip).wait_send()

    def drain(e, carry):
        valid, slot, flag = event(e)
        for direction in range(4):
            @pl.when(flag[direction])
            def _(direction=direction):
                hand_on(direction, slot).wait_send()
        return carry

    lax.fori_loop(0, EVENTS, drain, 0)
    for copy in x_copies + w_copies + s_copies:
        copy.wait_send()

    for j in range(1, 4):
        pltpu.make_async_remote_copy(
            src_ref=wout_hbm.at[:, columns], dst_ref=wcol.at[y_of[j]], send_sem=w_send.at[j],
            recv_sem=w_recv.at[y_of[j]], device_id=(seq, y_of[j]), device_id_type=MESH).wait_recv()
    for j in range(4):
        for c in range(2):
            if j == 0 and c == 0:
                continue
            lot_of = y_of[j] * 2 + (core if c == 0 else other)
            pltpu.make_async_remote_copy(
                src_ref=ogive.at[core], dst_ref=att.at[lot_of], send_sem=o_send.at[j * 2 + c],
                recv_sem=o_recv.at[lot_of], device_id=partner, device_id_type=MESH).wait_recv()

    total = None
    for y in range(4):
        both = jnp.concatenate([att[2 * y], att[2 * y + 1]], axis=1)
        term = jnp.dot(both, wcol[y], preferred_element_type=f32)
        total = term if total is None else total + term
    out_ref[...] = total.astype(bf16)

    for copy in o_copies:
        copy.wait_send()


def per_device(face_rows, norm_gain, w_qkv, w_out, segments):
    bf16, f32 = jnp.bfloat16, jnp.float32
    vmem = pl.BlockSpec(memory_space=pltpu.VMEM)
    hbm = pl.BlockSpec(memory_space=pl.ANY)
    dma = pltpu.SemaphoreType.DMA
    return pl.pallas_call(
        kernel,
        name="face_attention",
        out_shape=jax.ShapeDtypeStruct((ROWS, ROWS), bf16),
        in_specs=[hbm, vmem, hbm, hbm, vmem],
        out_specs=vmem,
        scratch_shapes=[
            pltpu.VMEM((4, ROWS, ROWS), bf16),
            pltpu.VMEM((3, 1024, ROWS), bf16),
            pltpu.VMEM((4, ROWS, ROWS), bf16),
            pltpu.VMEM((32, SLOT, HD), bf16),
            pltpu.VMEM((4, ROWS, HD), bf16),
            pltpu.VMEM((BLOCK, HD), bf16),
            pltpu.VMEM((BLOCK, HD), bf16),
            pltpu.VMEM((BLOCK, HD), f32),
            pltpu.VMEM((BLOCK, HD), f32),
            pltpu.VMEM((BLOCK, HD), f32),
            pltpu.VMEM((2, ROWS, HD), bf16),
            pltpu.VMEM((8, ROWS, HD), bf16),
            dma((3,)),
            dma((4,)), dma((4,)),
            dma((4,)), dma((4,)),
            dma((4,)), dma((4,)),
            dma((4, 32)), dma((32,)),
            dma((8,)), dma((8,)),
        ],
        compiler_params=pltpu.CompilerParams(
            collective_id=0, has_side_effects=True, vmem_limit_bytes=67043328),
    )(
        face_rows,
        norm_gain.reshape(1, 1024),
        jnp.transpose(w_qkv, (1, 0, 2)),
        w_out,
        segments.reshape(2, HD),
    )


def solution(mesh):
    in_specs = (P("seq", "head"), P(), P(None, None, "head"), P("head", None), P("seq"))
    out_specs = P("seq", "head")
    return jax.shard_map(
        per_device, mesh=mesh, in_specs=in_specs, out_specs=out_specs, check_vma=False
    )
```

```python
import functools
import math

import jax
import jax.numpy as jnp
from jax import lax
from jax.experimental import pallas as pl
from jax.experimental.pallas import tpu as pltpu
from jax.sharding import PartitionSpec as P

MESH = pl.DeviceIdType.MESH
HD = 128
epsilon = 1e-05
masked_score = -1e30
PLAN = (
    (1131137, 734113, 1075723, 683, 0, 0, 0, 0, 0, 0, 0, 0, 0, 0, 0, 0, 0, 0, 0, 103),
    (1134656, 1073803, 2294054, 2731, 2049, 2049, 2049, 2049, 2049, 2049, 2049, 2049, 2049, 2049, 2049, 2049, 2049, 2049, 2049, 255),
    (657962, 2820747, 131755, 2163340, 4098, 4098, 4098, 4098, 4098, 4098, 4098, 4098, 4098, 4098, 4098, 4098, 4098, 4098, 4098, 221),
    (660107, 2298539, 600204, 2296129, 2162688, 6147, 6147, 6147, 6147, 6147, 6147, 6147, 6147, 6147, 6147, 6147, 6147, 6147, 6147, 85),
    (137868, 2824613, 2822466, 2689281, 2949120, 8196, 8196, 8196, 8196, 8196, 8196, 8196, 8196, 8196, 8196, 8196, 8196, 8196, 8196, 93),
    (2826564, 2300227, 786727, 2424898, 3426, 11297, 10245, 10245, 10245, 10245, 10245, 10245, 10245, 10245, 10245, 10245, 10245, 10245, 10245, 188),
    (731559, 664111, 1091712, 2303392, 265285, 2824259, 660641, 13346, 12294, 12294, 12294, 12294, 12294, 12294, 12294, 12294, 12294, 12294, 12294, 85),
    (786694, 2425391, 265574, 2427173, 8269, 2108708, 530731, 2168834, 15394, 14343, 14343, 14343, 14343, 14343, 14343, 14343, 14343, 14343, 14343, 228),
    (280640, 611808, 346183, 2308257, 2175302, 858242, 667042, 2103556, 2171905, 17445, 16392, 16392, 16392, 16392, 16392, 16392, 16392, 16392, 16392, 246),
    (2730, 2164840, 655490, 2246240, 7586, 2308423, 734371, 2240772, 601124, 19461, 18441, 18441, 18441, 18441, 18441, 18441, 18441, 18441, 18441, 119),
    (266569, 2430057, 2435, 2431272, 2295872, 795744, 2958344, 862279, 603239, 2110469, 20490, 20490, 20490, 20490, 20490, 20490, 20490, 20490, 20490, 245),
    (268362, 2839971, 270338, 2312521, 339108, 3205, 536576, 2167841, 2164006, 16647, 2180391, 22539, 22539, 22539, 22539, 22539, 22539, 22539, 22539, 153),
    (270667, 2958635, 2697605, 2314570, 798819, 2428994, 216486, 133383, 2297097, 279555, 66855, 2098472, 24588, 24588, 24588, 24588, 24588, 24588, 24588, 93),
    (680133, 9324, 153990, 2172070, 801829, 675971, 2963592, 19491, 2707584, 2966560, 2101346, 2181121, 2165803, 26637, 26637, 26637, 26637, 26637, 26637, 85),
    (158086, 2189871, 1093030, 1190279, 2178085, 680328, 2441284, 805932, 2181280, 2097483, 20515, 4129, 2167844, 2184193, 2186243, 28686, 28686, 28686, 28686, 69),
    (553415, 2441608, 1600615, 804934, 263337, 207904, 25669, 4164, 546977, 2190820, 21697, 400554, 3216430, 2188323, 2176043, 30735, 30735, 30735, 30735, 228),
    (821576, 228584, 870833, 873807, 212106, 749600, 143489, 2164738, 7502, 747691, 2640995, 2167819, 2124076, 205964, 2106368, 2176007, 2172933, 32784, 32784, 119),
    (2326608, 807401, 1196338, 687497, 2848898, 2183201, 212008, 2243585, 284803, 24942, 2782636, 262150, 2438178, 337924, 2123821, 2169861, 2171947, 34833, 34833, 119),
    (690314, 267306, 19825, 689186, 2313520, 286731, 147651, 2974824, 2168900, 556075, 2324749, 80996, 2111525, 2369838, 2713638, 2110478, 36882, 36882, 36882, 117),
    (811122, 2266540, 2787697, 217251, 557453, 553065, 272395, 2452489, 274984, 2245642, 621611, 2128934, 9219, 2171950, 80944, 2112549, 38931, 38931, 38931, 85),
    (287059, 3104772, 814451, 22926, 2316402, 2171950, 818349, 273746, 557105, 2788517, 2719882, 13354, 2194470, 14377, 2178121, 2179080, 40980, 40980, 40980, 85),
    (565645, 2977934, 1125869, 818548, 295251, 2332780, 2982002, 2456581, 14374, 1268775, 2265096, 35852, 2722822, 21515, 2180138, 2181129, 43029, 43029, 43029, 85),
    (815383, 3109461, 818549, 223376, 239024, 341167, 24615, 2318675, 2112518, 559240, 2858417, 2443273, 284714, 103437, 2139146, 2180651, 46098, 45078, 45078, 85),
    (948502, 2324880, 2732103, 1275312, 2570517, 344209, 2114869, 1397838, 347569, 2386541, 2117514, 1050932, 37139, 204811, 2200108, 2186291, 2122772, 47127, 47127, 70),
    (313424, 1050809, 2340951, 1116305, 177201, 30866, 86057, 2194610, 2326536, 1136819, 1207414, 95272, 2137099, 2126348, 40981, 2118765, 2206772, 2188297, 49176, 51),
    (180737, 300152, 84513, 1071658, 367794, 2398295, 2248753, 3233940, 287863, 2203734, 2115695, 94224, 1076342, 2467861, 2196524, 2128913, 2190350, 51225, 51225, 51),
    (430594, 1118297, 2331769, 34858, 1071251, 2463832, 3234936, 304177, 2465804, 305264, 30743, 2130988, 2468874, 2340877, 28694, 2208815, 2190382, 53274, 53274, 17),
    (301146, 304307, 2347531, 38443, 25780, 2187413, 34905, 2468985, 46194, 27761, 181302, 32910, 3241080, 48688, 31863, 2190383, 55323, 55323, 55323, 17),
    (303620, 2349147, 40116, 184469, 2468979, 307244, 2348214, 116910, 354455, 168079, 101490, 2126861, 2280460, 2131984, 2146360, 2196527, 58423, 57372, 57372, 17),
    (188933, 1124501, 2468988, 186518, 2469901, 172056, 357499, 2211930, 310445, 105588, 31758, 2456698, 117779, 34864, 2129938, 2210866, 2198553, 59421, 59421, 17),
    (307293, 2354358, 188568, 310456, 2351246, 2192047, 186421, 2140185, 2129081, 99451, 1220698, 296979, 2473104, 2198580, 2201618, 2348082, 61470, 61470, 61470, 17),
    (178328, 1128478, 2604216, 177214, 59545, 2222191, 2477071, 294940, 2338833, 56380, 2196114, 3510357, 2219061, 2197555, 151578, 3186804, 2216979, 63519, 63519, 0),
    (854568, 1132673, 266402, 1135366, 65568, 65568, 65568, 65568, 65568, 65568, 65568, 65568, 65568, 65568, 65568, 65568, 65568, 65568, 65568, 247),
    (1133474, 197129, 2752642, 1397027, 68364, 67617, 67617, 67617, 67617, 67617, 67617, 67617, 67617, 67617, 67617, 67617, 67617, 67617, 67617, 127),
    (334378, 2754913, 2228576, 1077900, 69666, 69666, 69666, 69666, 69666, 69666, 69666, 69666, 69666, 69666, 69666, 69666, 69666, 69666, 69666, 119),
    (725515, 1649986, 199181, 66188, 2622094, 72769, 71715, 71715, 71715, 71715, 71715, 71715, 71715, 71715, 71715, 71715, 71715, 71715, 71715, 223),
    (727205, 2759180, 1143437, 2232674, 199310, 2230304, 75008, 73764, 73764, 73764, 73764, 73764, 73764, 73764, 73764, 73764, 73764, 73764, 73764, 85),
    (1337700, 2237102, 727182, 853059, 2101602, 68992, 77121, 75813, 75813, 75813, 75813, 75813, 75813, 75813, 75813, 75813, 75813, 75813, 75813, 87),
    (731687, 1340078, 328773, 1079396, 2884932, 2759011, 528417, 2624802, 77862, 77862, 77862, 77862, 77862, 77862, 77862, 77862, 77862, 77862, 77862, 92),
    (1341856, 2883654, 330021, 2624517, 69668, 2888742, 597252, 80899, 79911, 79911, 79911, 79911, 79911, 79911, 79911, 79911, 79911, 79911, 79911, 70),
    (1919328, 735393, 281927, 857345, 348230, 2831360, 732162, 532618, 2696453, 2103331, 81960, 81960, 81960, 81960, 81960, 81960, 81960, 81960, 81960, 123),
    (738218, 2244641, 66945, 2097314, 2887843, 2242663, 337027, 548934, 77158, 2632836, 84009, 84009, 84009, 84009, 84009, 84009, 84009, 84009, 84009, 191),
    (739618, 2364681, 213283, 2244705, 2366529, 604324, 2367584, 601415, 668805, 2176000, 86058, 86058, 86058, 86058, 86058, 86058, 86058, 86058, 86058, 91),
    (1073315, 2365802, 740682, 135588, 2168196, 2893989, 2408, 262182, 2296840, 2294023, 2110537, 89127, 88107, 88107, 88107, 88107, 88107, 88107, 88107, 213),
    (219437, 2498980, 601163, 217123, 2235525, 865610, 84002, 2233350, 342312, 97, 2163719, 2640904, 91137, 90156, 90156, 90156, 90156, 90156, 90156, 245),
    (862510, 3025260, 2253103, 340068, 2105707, 2776454, 606243, 151591, 2103392, 69929, 2898944, 2315266, 2117000, 2164865, 92205, 92205, 92205, 92205, 92205, 147),
    (471471, 3027309, 2779560, 108, 870437, 2238564, 2177415, 2254216, 2902123, 69699, 2250785, 87075, 2100234, 2163716, 95234, 94254, 94254, 94254, 94254, 155),
    (868455, 3029294, 66574, 346413, 2097766, 208141, 331144, 2378753, 528684, 87074, 2105380, 2118725, 2110476, 88099, 2104331, 96303, 96303, 96303, 96303, 134),
    (671921, 65809, 752640, 2179241, 67687, 1856583, 547118, 144385, 70827, 2176170, 2129033, 747621, 71724, 2782477, 2102275, 2107396, 2171916, 98352, 98352, 99),
    (330096, 2183306, 809064, 2448456, 2130057, 876583, 135535, 2365603, 2167809, 74764, 2259975, 92198, 76841, 95236, 2126853, 2110477, 100401, 100401, 100401, 119),
    (807025, 2787499, 71051, 2183536, 2246697, 82348, 2365603, 2131016, 751661, 335911, 881676, 2368514, 11271, 2126885, 2385926, 2176015, 102450, 102450, 102450, 85),
    (758187, 2790603, 876579, 217201, 2264195, 2121833, 878896, 2117796, 2498734, 2173061, 2244648, 3164199, 621581, 341008, 2110535, 2128910, 104499, 104499, 104499, 85),
    (759980, 2516243, 758189, 357714, 624746, 88743, 96292, 2250065, 85003, 2123920, 2371750, 76942, 83248, 2391045, 2114564, 2112521, 106548, 106548, 106548, 85),
    (2793844, 77998, 90149, 26995, 1391692, 758917, 819631, 2265195, 2651270, 2250794, 2268592, 2914344, 2189649, 2112522, 2114609, 2181129, 108597, 108597, 108597, 85),
    (174246, 1522997, 2109812, 2793616, 2519086, 761008, 292877, 2111858, 16460, 625938, 2189387, 2193545, 21544, 2182186, 2186284, 2137105, 110646, 110646, 110646, 84),
    (885103, 2392342, 886824, 225301, 79913, 2111796, 2128950, 224532, 2257997, 2205834, 105480, 2132140, 135211, 103594, 2253833, 2120722, 113683, 112695, 112695, 68),
    (1048761, 1130704, 243865, 2113722, 298071, 96297, 1061897, 241842, 3308074, 367762, 2143242, 2195467, 109715, 2271342, 107569, 224299, 91156, 2122765, 115726, 51),
    (245946, 1116273, 1119320, 99345, 364585, 3311241, 2396339, 243754, 23639, 2399242, 1210486, 2447532, 2194572, 108596, 2125870, 27669, 2143277, 117780, 116793, 51),
    (364665, 2396714, 367705, 2379889, 181395, 2264184, 1212587, 2119735, 1073332, 2401328, 371756, 2275982, 97301, 2192013, 2190415, 2404406, 118842, 118842, 118842, 19),
    (367139, 1054842, 2399322, 368875, 102521, 2401291, 1125394, 371801, 1337452, 2122901, 94257, 49206, 99342, 2452536, 2132023, 2405392, 97303, 121935, 120891, 17),
    (252084, 2284692, 370700, 249907, 1076314, 2268309, 356907, 116918, 2280557, 103950, 375852, 2405458, 2132081, 114735, 33815, 2147376, 123919, 122940, 122940, 17),
    (370812, 2534492, 373261, 106619, 2283566, 118967, 2281523, 3316886, 377007, 102425, 3239063, 2134577, 2214096, 2127000, 2128944, 2133012, 124989, 124989, 124989, 17),
    (256550, 1128694, 254478, 376366, 240790, 377359, 2407509, 41083, 379996, 105524, 2194584, 119899, 2288730, 102448, 2137106, 35865, 2130993, 127038, 127038, 17),
    (127223, 378071, 2408623, 2158777, 3308150, 32829, 2274544, 2410682, 123509, 2271889, 2328626, 2269300, 3183644, 1087547, 2202651, 2157594, 129087, 129087, 129087, 0),
)
EVENTS = 2 * (len(PLAN[0]) - 1)
ROWS = 256
BLOCK = 512
INFO = 16
SLOT = 2 * ROWS + INFO


def pick(values, index):
    result = jnp.int32(values[0])
    for at in range(1, len(values)):
        result = jnp.where(index == at, jnp.int32(values[at]), result)
    return result


def kernel(
    x_hbm, gain_hbm, wqkv_hbm, wout_hbm, seg_hbm, out_ref,
    xbuf, gain_ref, wqkv, wcol, seg_ref, kv, give, qgive, qrows, qmask, acc, run_max, run_sum, ogive, att,
    local_sem, x_send, x_recv, w_send, w_recv, s_send, s_recv, kv_send, kv_recv, o_send, o_recv,
):
    f32, bf16 = jnp.float32, jnp.bfloat16
    seq, head = lax.axis_index("seq"), lax.axis_index("head")
    core = lax.rem(seq, 2)
    chip = lax.div(seq, 2)
    z = lax.rem(chip, 8)
    x = lax.div(chip, 8)
    other = 1 - core

    def at(xx, zz, cc):
        return (xx * 8 + zz) * 2 + cc

    z_up, z_down = lax.rem(z + 1, 8), lax.rem(z + 7, 8)
    x_up, x_down = lax.rem(x + 1, 4), lax.rem(x + 3, 4)
    up = (at(x, z_up, core), head)
    down = (at(x, z_down, core), head)
    right = (at(x_up, z, core), head)
    left = (at(x_down, z, core), head)
    partner = (at(x, z, other), head)
    y_of = [lax.rem(head + j, 4) for j in range(4)]

    barrier = pltpu.get_barrier_semaphore()
    greeted = [up, down, right, left, partner]
    for j in range(1, 4):
        greeted.append((seq, y_of[j]))
        greeted.append((at(x, z, other), y_of[j]))
    for device in greeted:
        pl.semaphore_signal(barrier, inc=1, device_id=device, device_id_type=MESH)

    seg_in = pltpu.make_async_copy(seg_hbm, seg_ref, local_sem.at[3])
    seg_in.start()
    gain_in = pltpu.make_async_copy(gain_hbm, gain_ref, local_sem.at[4])
    gain_in.start()
    mine = pltpu.make_async_copy(x_hbm, xbuf.at[head], local_sem.at[0])
    mine.start()
    weights_in = pltpu.make_async_copy(wqkv_hbm, wqkv, local_sem.at[1])
    weights_in.start()
    columns = pl.ds(pl.multiple_of(head * ROWS, ROWS), ROWS)
    wcol_in = pltpu.make_async_copy(wout_hbm.at[:, columns], wcol.at[head], local_sem.at[2])
    wcol_in.start()

    seg_in.wait()
    seg = seg_ref[...]
    lane = lax.broadcasted_iota(jnp.int32, (1, HD), 1)
    sub = lax.broadcasted_iota(jnp.int32, (INFO, HD), 0)
    lower = jnp.zeros((1, HD), f32)
    upper = jnp.zeros((1, HD), f32)
    for t in range(1, 5):
        before = jnp.sum(jnp.where(seg < t, 1.0, 0.0).astype(f32), axis=1, keepdims=True)
        before = before[0:1] + before[1:2]
        lower = jnp.where(lane == t, before, lower)
        upper = jnp.where(lane == t - 1, before, upper)
    lower = jnp.where(lane < 4, lower, 0.0)
    info = jnp.where(sub == 0, lower, jnp.where(sub == 1, upper, 0.0)).astype(bf16)

    mine_at = core * 32 + chip
    words = [pick([row[i] for row in PLAN], mine_at) for i in range(len(PLAN[0]))]
    pl.semaphore_wait(barrier, len(greeted))

    x_copies = []
    for j in range(1, 4):
        copy = pltpu.make_async_remote_copy(
            src_ref=x_hbm, dst_ref=xbuf.at[head], send_sem=x_send.at[j], recv_sem=x_recv.at[head],
            device_id=(seq, y_of[j]), device_id_type=MESH)
        copy.start()
        x_copies.append(copy)
    gain_in.wait()
    mine.wait()
    weights_in.wait()
    wcol_in.wait()
    for j in range(1, 4):
        pltpu.make_async_remote_copy(
            src_ref=x_hbm, dst_ref=xbuf.at[y_of[j]], send_sem=x_send.at[j], recv_sem=x_recv.at[y_of[j]],
            device_id=(seq, y_of[j]), device_id_type=MESH).wait_recv()

    w_copies = []
    for j in range(1, 4):
        theirs = pl.ds(pl.multiple_of(y_of[j] * ROWS, ROWS), ROWS)
        copy = pltpu.make_async_remote_copy(
            src_ref=wout_hbm.at[:, theirs], dst_ref=wcol.at[head], send_sem=w_send.at[j],
            recv_sem=w_recv.at[head], device_id=(seq, y_of[j]), device_id_type=MESH)
        copy.start()
        w_copies.append(copy)

    squares = jnp.zeros((ROWS, 1), f32)
    for y in range(4):
        part = xbuf[y].astype(f32)
        squares = squares + jnp.sum(part * part, axis=1, keepdims=True)
    scale = lax.rsqrt(squares * (1.0 / 1024.0) + epsilon)
    normed = []
    for y in range(4):
        gain = gain_ref[:, y * ROWS : (y + 1) * ROWS]
        normed.append((xbuf[y].astype(f32) * scale * gain).astype(bf16))

    def project(which):
        total = None
        for y in range(4):
            term = jnp.dot(
                normed[y], wqkv[which, y * ROWS : (y + 1) * ROWS, :], preferred_element_type=f32)
            total = term if total is None else total + term
        return total

    def hand_on(direction, piece):
        device = (up, down, right, left)[direction]
        return pltpu.make_async_remote_copy(
            src_ref=kv.at[piece], dst_ref=kv.at[piece], send_sem=kv_send.at[direction, piece],
            recv_sem=kv_recv.at[piece], device_id=device, device_id_type=MESH)

    own = pl.ds(pl.multiple_of(core * ROWS, ROWS), ROWS)
    own_piece = core * 32 + chip
    other_piece = other * 32 + chip

    def swap(j, source, target, landing):
        return pltpu.make_async_remote_copy(
            src_ref=source, dst_ref=target, send_sem=s_send.at[j], recv_sem=landing,
            device_id=partner, device_id_type=MESH)

    give[2 * ROWS : SLOT, :] = info
    kv[own_piece, 2 * ROWS : SLOT, :] = info
    for j in (1, 2):
        both = project(j).astype(bf16)
        first, second = both[:, :HD], both[:, HD:]
        give[(j - 1) * ROWS : j * ROWS, :] = jnp.where(core == 0, second, first)
        kv[own_piece, (j - 1) * ROWS : j * ROWS, :] = jnp.where(core == 0, first, second)

    own_flag = [lax.rem(lax.div(words[-1], 1 << i), 2) == 1 for i in range(8)]
    s_copies = [swap(0, give, kv.at[own_piece], kv_recv.at[own_piece])]
    s_copies[0].start()
    for direction in range(4):
        @pl.when(own_flag[direction])
        def _(direction=direction):
            hand_on(direction, own_piece).start()

    both = (project(0) * (1.0 / math.sqrt(HD))).astype(bf16)
    first, second = both[:, :HD], both[:, HD:]
    qgive[...] = jnp.where(core == 0, second, first)
    s_copies.append(swap(1, qgive, qrows.at[own], s_recv.at[1]))
    s_copies[1].start()
    qrows[own, :] = jnp.where(core == 0, first, second)

    swap(0, give, kv.at[other_piece], kv_recv.at[other_piece]).wait_recv()
    for direction in range(4):
        @pl.when(own_flag[4 + direction])
        def _(direction=direction):
            hand_on(direction, other_piece).start()
    s_copies[1].wait_recv()

    def event(e):
        pair = lax.div(e, 2)
        word = words[0]
        for i in range(1, len(words) - 1):
            word = jnp.where(pair == i, words[i], word)
        code = jnp.where(lax.rem(e, 2) == 0, lax.rem(word, 2048), lax.div(word, 2048))
        piece = lax.rem(code, 64)
        flag = [lax.rem(lax.div(code, 64 << i), 2) == 1 for i in range(5)]
        source = lax.rem(piece, 32)
        return source != chip, piece, source, flag

    row = lax.broadcasted_iota(jnp.int32, (ROWS, HD), 0).astype(f32)
    lanes = lax.broadcasted_iota(jnp.int32, (ROWS, HD), 1)

    def inside(piece):
        bounds = kv[piece, 2 * ROWS : SLOT, :].astype(f32)
        return (row >= bounds[0:1, :]) & (row < bounds[1:2, :])

    for half in range(2):
        qmask[half * ROWS : (half + 1) * ROWS, :] = jnp.where(
            inside(half * 32 + chip) | (lanes >= 4), 0.0, masked_score).astype(bf16)

    def keys_of(piece):
        return jnp.concatenate(
            [kv[piece, 0:ROWS, :], jnp.where(inside(piece), 1.0, 0.0).astype(bf16)], axis=1)

    def scores_of(part, keys):
        rows = slice(part * ROWS, (part + 1) * ROWS)
        queries = jnp.concatenate([qrows[rows, :], qmask[rows, :]], axis=1)
        return lax.dot_general(queries, keys, (((1,), (1,)), ((), ())), preferred_element_type=f32)

    def keep(part, new_max, total, product):
        rows = slice(part * ROWS, (part + 1) * ROWS)
        run_max[rows, :] = jnp.broadcast_to(new_max, (ROWS, HD))
        run_sum[rows, :] = jnp.broadcast_to(total, (ROWS, HD))
        acc[rows, :] = product

    own_keys = [keys_of(chip), keys_of(32 + chip)]
    own_values = [kv[half * 32 + chip, ROWS : 2 * ROWS, :] for half in range(2)]
    q_at = lax.broadcasted_iota(jnp.int32, (ROWS, ROWS), 0)
    k_at = lax.broadcasted_iota(jnp.int32, (ROWS, ROWS), 1)
    for part in range(2):
        scores = [scores_of(part, own_keys[half]) for half in range(part + 1)]
        scores[part] = jnp.where(k_at <= q_at, scores[part], masked_score)
        new_max = jnp.max(scores[part], axis=1, keepdims=True)
        if part == 1:
            new_max = jnp.maximum(new_max, jnp.max(scores[0], axis=1, keepdims=True))
        total, product = 0.0, 0.0
        for half in range(part + 1):
            weights = jnp.exp(scores[half] - new_max)
            total = total + jnp.sum(weights, axis=1, keepdims=True)
            product = product + jnp.dot(
                weights.astype(bf16), own_values[half], preferred_element_type=f32)
        keep(part, new_max, total, product)

    def attend(source):
        keys = jnp.concatenate([keys_of(source), keys_of(32 + source)], axis=0)
        values = jnp.concatenate(
            [kv[half * 32 + source, ROWS : 2 * ROWS, :] for half in range(2)], axis=0)
        for part in range(2):
            rows = slice(part * ROWS, (part + 1) * ROWS)
            scores = scores_of(part, keys)
            old_max = run_max[rows, 0:1]
            new_max = jnp.maximum(old_max, jnp.max(scores, axis=1, keepdims=True))
            weights = jnp.exp(scores - new_max)
            factor = jnp.exp(old_max - new_max)
            total = run_sum[rows, 0:1] * factor + jnp.sum(weights, axis=1, keepdims=True)
            product = acc[rows, :] * factor + jnp.dot(
                weights.astype(bf16), values, preferred_element_type=f32)
            keep(part, new_max, total, product)

    def step(e, carry):
        valid, piece, source, flag = event(e)

        @pl.when(valid)
        def _():
            hand_on(0, piece).wait_recv()
            for direction in range(4):
                @pl.when(flag[direction])
                def _(direction=direction):
                    hand_on(direction, piece).start()

            @pl.when(flag[4])
            def _():
                attend(source)

        return carry

    lax.fori_loop(0, EVENTS, step, 0)

    for half in range(2):
        rows = slice(half * ROWS, (half + 1) * ROWS)
        ogive[half] = (acc[rows, :] / run_sum[rows, 0:1]).astype(bf16)

    o_copies = []
    lot = head * 2 + core
    for j in range(4):
        for c in range(2):
            if j == 0 and c == 0:
                continue
            row_core = core if c == 0 else other
            copy = pltpu.make_async_remote_copy(
                src_ref=ogive.at[row_core], dst_ref=att.at[lot], send_sem=o_send.at[j * 2 + c],
                recv_sem=o_recv.at[lot], device_id=(at(x, z, row_core), y_of[j]), device_id_type=MESH)
            copy.start()
            o_copies.append(copy)
    att[lot] = ogive[core]

    for direction in range(8):
        @pl.when(own_flag[direction])
        def _(direction=direction):
            hand_on(direction % 4, own_piece if direction < 4 else other_piece).wait_send()

    def drain(e, carry):
        valid, piece, source, flag = event(e)
        for direction in range(4):
            @pl.when(flag[direction])
            def _(direction=direction):
                hand_on(direction, piece).wait_send()
        return carry

    lax.fori_loop(0, EVENTS, drain, 0)
    for copy in x_copies + w_copies + s_copies:
        copy.wait_send()

    for j in range(1, 4):
        pltpu.make_async_remote_copy(
            src_ref=wout_hbm.at[:, columns], dst_ref=wcol.at[y_of[j]], send_sem=w_send.at[j],
            recv_sem=w_recv.at[y_of[j]], device_id=(seq, y_of[j]), device_id_type=MESH).wait_recv()
    for j in range(4):
        for c in range(2):
            if j == 0 and c == 0:
                continue
            lot_of = y_of[j] * 2 + (core if c == 0 else other)
            pltpu.make_async_remote_copy(
                src_ref=ogive.at[core], dst_ref=att.at[lot_of], send_sem=o_send.at[j * 2 + c],
                recv_sem=o_recv.at[lot_of], device_id=partner, device_id_type=MESH).wait_recv()

    total = None
    for y in range(4):
        both = jnp.concatenate([att[2 * y], att[2 * y + 1]], axis=1)
        term = jnp.dot(both, wcol[y], preferred_element_type=f32)
        total = term if total is None else total + term
    out_ref[...] = total.astype(bf16)

    for copy in o_copies:
        copy.wait_send()


def per_device(face_rows, norm_gain, w_qkv, w_out, segments):
    bf16, f32 = jnp.bfloat16, jnp.float32
    vmem = pl.BlockSpec(memory_space=pltpu.VMEM)
    hbm = pl.BlockSpec(memory_space=pl.ANY)
    dma = pltpu.SemaphoreType.DMA
    return pl.pallas_call(
        kernel,
        name="face_attention",
        out_shape=jax.ShapeDtypeStruct((ROWS, ROWS), bf16),
        in_specs=[hbm, hbm, hbm, hbm, hbm],
        out_specs=vmem,
        scratch_shapes=[
            pltpu.VMEM((4, ROWS, ROWS), bf16),
            pltpu.VMEM((1, 1024), f32),
            pltpu.VMEM((3, 1024, ROWS), bf16),
            pltpu.VMEM((4, ROWS, ROWS), bf16),
            pltpu.VMEM((2, HD), jnp.int32),
            pltpu.VMEM((64, SLOT, HD), bf16),
            pltpu.VMEM((SLOT, HD), bf16),
            pltpu.VMEM((ROWS, HD), bf16),
            pltpu.VMEM((BLOCK, HD), bf16),
            pltpu.VMEM((BLOCK, HD), bf16),
            pltpu.VMEM((BLOCK, HD), f32),
            pltpu.VMEM((BLOCK, HD), f32),
            pltpu.VMEM((BLOCK, HD), f32),
            pltpu.VMEM((2, ROWS, HD), bf16),
            pltpu.VMEM((8, ROWS, HD), bf16),
            dma((5,)),
            dma((4,)), dma((4,)),
            dma((4,)), dma((4,)),
            dma((4,)), dma((4,)),
            dma((4, 64)), dma((64,)),
            dma((8,)), dma((8,)),
        ],
        compiler_params=pltpu.CompilerParams(
            collective_id=0, has_side_effects=True, vmem_limit_bytes=67043328),
    )(
        face_rows,
        norm_gain.reshape(1, 1024),
        jnp.transpose(w_qkv, (1, 0, 2)),
        w_out,
        segments.reshape(2, HD),
    )


def solution(mesh):
    in_specs = (P("seq", "head"), P(), P(None, None, "head"), P("head", None), P("seq"))
    out_specs = P("seq", "head")
    return jax.shard_map(
        per_device, mesh=mesh, in_specs=in_specs, out_specs=out_specs, check_vma=False
    )
```

```python
import functools
import math

import jax
import jax.numpy as jnp
from jax import lax
from jax.experimental import pallas as pl
from jax.experimental.pallas import tpu as pltpu
from jax.sharding import PartitionSpec as P

MESH = pl.DeviceIdType.MESH
HD = 128
epsilon = 1e-05
masked_score = -1e30
PLAN = (
    (1130881, 854311, 1147408, 856450, 1069862, 1274019, 1075883, 557, 0, 0, 0, 0, 0, 0, 0, 0, 0, 0, 0, 183),
    (1133065, 131202, 1069474, 2293923, 1399313, 2606, 2049, 2049, 2049, 2049, 2049, 2049, 2049, 2049, 2049, 2049, 2049, 2049, 2049, 183),
    (858177, 1071658, 1400161, 1083456, 1154400, 4652, 4098, 4098, 4098, 4098, 4098, 4098, 4098, 4098, 4098, 4098, 4098, 4098, 4098, 183),
    (660107, 1073835, 1401954, 1085697, 2820653, 2818048, 6147, 6147, 6147, 6147, 6147, 6147, 6147, 6147, 6147, 6147, 6147, 6147, 6147, 189),
    (662156, 1075884, 1404259, 1077314, 1158434, 1085793, 1079296, 2100256, 8753, 8196, 8196, 8196, 8196, 8196, 8196, 8196, 8196, 8196, 8196, 85),
    (664077, 1141262, 605284, 371246, 1079619, 263459, 237826, 2162945, 2692129, 10245, 10245, 10245, 10245, 10245, 10245, 10245, 10245, 10245, 10245, 221),
    (1915205, 2828974, 663936, 2827424, 137601, 1156129, 2429186, 13347, 12294, 12294, 12294, 12294, 12294, 12294, 12294, 12294, 12294, 12294, 12294, 212),
    (209280, 11680, 2427265, 2110501, 532610, 2172322, 612515, 1090563, 14343, 14343, 14343, 14343, 14343, 14343, 14343, 14343, 14343, 14343, 14343, 180),
    (655888, 346672, 1855745, 2308423, 2427438, 266566, 2306435, 2168227, 1075204, 2163565, 666788, 17701, 16392, 16392, 16392, 16392, 16392, 16392, 16392, 247),
    (1331457, 213521, 132424, 268546, 146851, 2162820, 2958439, 2167841, 616454, 2175045, 19749, 18441, 18441, 18441, 18441, 18441, 18441, 18441, 18441, 189),
    (673922, 1084777, 1153155, 2299299, 67944, 2244996, 2433088, 146464, 863233, 537639, 2632998, 20490, 20490, 20490, 20490, 20490, 20490, 20490, 20490, 151),
    (548938, 1085571, 271466, 673858, 2313636, 11299, 2959553, 274440, 132200, 556065, 2961735, 2168103, 23584, 22539, 22539, 22539, 22539, 22539, 22539, 157),
    (678413, 1665412, 1602788, 7275, 675973, 2839717, 275491, 1866258, 149538, 2962537, 2296321, 82343, 2114562, 561, 2112544, 24588, 24588, 24588, 24588, 223),
    (273294, 2435404, 8582, 1342828, 2437451, 2171303, 803847, 138603, 2168842, 4096, 2180202, 2057, 2165920, 2299177, 26637, 26637, 26637, 26637, 26637, 191),
    (682438, 294118, 142701, 802828, 2304391, 2844072, 84096, 677892, 2172064, 21803, 2164737, 7274, 2116647, 2168834, 29730, 28686, 28686, 28686, 28686, 215),
    (932232, 2846734, 1192, 870982, 158944, 283687, 2174977, 2845857, 4628, 532549, 2377731, 2167909, 25763, 2187307, 2120740, 31786, 30735, 30735, 30735, 70),
    (541073, 886880, 2572623, 365935, 280577, 145546, 70759, 685089, 2097587, 13353, 2102374, 2184302, 350243, 877635, 2646061, 2644037, 2123812, 2106405, 32784, 187),
    (561289, 164274, 1379696, 2099744, 890952, 2494626, 2179407, 71722, 2118767, 2181388, 2242663, 468396, 551182, 2906155, 2190382, 78851, 2105381, 2108422, 34833, 59),
    (676433, 1381043, 689265, 2850825, 2445315, 812137, 148515, 285868, 2310415, 2101645, 2848964, 2189351, 2185253, 2171911, 274446, 2176046, 37893, 36882, 36882, 115),
    (23122, 2855043, 3217548, 560300, 21739, 2852937, 813328, 204805, 2452848, 17513, 2172934, 816232, 2454532, 2175087, 15375, 2178090, 38931, 38931, 38931, 117),
    (2857299, 22700, 272525, 2122322, 2174258, 2185350, 2189454, 8753, 149578, 2577444, 31790, 99369, 17446, 2133008, 15400, 2178095, 40980, 40980, 40980, 85),
    (289108, 2859141, 155662, 2173011, 2857094, 2188334, 2176045, 22866, 80272, 31792, 821384, 21547, 2199561, 2315399, 2194472, 2198569, 43029, 43029, 43029, 85),
    (174414, 2454901, 555174, 2109780, 80272, 2334797, 2190768, 16460, 694417, 2722951, 2442547, 85167, 2187602, 154674, 21513, 2315307, 45078, 45078, 45078, 85),
    (948502, 2732432, 2849968, 1259598, 821269, 2729992, 2112945, 2191892, 27688, 364777, 2729609, 1204362, 2136115, 140333, 89106, 2120748, 48170, 47127, 47127, 68),
    (1114265, 82007, 163857, 2114679, 176274, 2458737, 31922, 2193958, 2338825, 2181130, 3232302, 1136725, 367669, 2126995, 1075220, 2190388, 2121772, 50187, 49176, 51),
    (1116248, 431224, 281778, 3491888, 348247, 3167248, 34963, 2329719, 31275, 45204, 2338926, 2187276, 2204750, 2123821, 2202635, 2193461, 52245, 51225, 51225, 19),
    (1118297, 2345010, 2118314, 180371, 33291, 2196600, 34964, 2135091, 2466859, 178188, 2341932, 161813, 2197677, 95245, 46319, 2468982, 54286, 53274, 53274, 17),
    (184835, 22675, 2347555, 3233940, 182284, 103604, 167033, 306220, 180909, 2202642, 308273, 2124981, 33912, 47662, 31856, 2126903, 2208879, 55323, 55323, 17),
    (303195, 2465804, 306299, 185388, 26707, 2189861, 2348083, 307214, 2467865, 233495, 3503225, 2134033, 31798, 2209880, 99384, 2198544, 58415, 57372, 57372, 17),
    (188933, 1386709, 27957, 308348, 309339, 3237902, 631931, 2471086, 2471955, 2201690, 115215, 52346, 37908, 296562, 2346031, 2146321, 2197041, 59421, 59421, 17),
    (190614, 309798, 2471037, 188967, 94232, 175118, 2206903, 2352312, 313359, 41051, 3505275, 2457616, 184337, 2347027, 2460724, 2201650, 2135161, 61470, 61470, 17),
    (61655, 1128600, 2475255, 177214, 313359, 32797, 2339901, 58543, 296978, 2195541, 2221173, 56370, 2219057, 2138228, 104474, 2137146, 64569, 63519, 63519, 0),
    (330280, 332582, 537097, 1069186, 1075757, 65568, 65568, 65568, 65568, 65568, 65568, 65568, 65568, 65568, 65568, 65568, 65568, 65568, 65568, 127),
    (856416, 266793, 1070400, 68139, 67617, 67617, 67617, 67617, 67617, 67617, 67617, 67617, 67617, 67617, 67617, 67617, 67617, 67617, 67617, 91),
    (596522, 1136993, 1072193, 721156, 70976, 69666, 69666, 69666, 69666, 69666, 69666, 69666, 69666, 69666, 69666, 69666, 69666, 69666, 69666, 127),
    (201092, 1140034, 723468, 66881, 72768, 71715, 71715, 71715, 71715, 71715, 71715, 71715, 71715, 71715, 71715, 71715, 71715, 71715, 71715, 87),
    (1583203, 724291, 2756898, 1145363, 2754592, 75008, 73764, 73764, 73764, 73764, 73764, 73764, 73764, 73764, 73764, 73764, 73764, 73764, 73764, 181),
    (729645, 728132, 2759343, 592439, 327682, 1154048, 2168065, 76304, 75813, 75813, 75813, 75813, 75813, 75813, 75813, 75813, 75813, 75813, 75813, 245),
    (731694, 1408069, 205216, 2884279, 68676, 727567, 2759189, 1081908, 1149346, 1154306, 78849, 77862, 77862, 77862, 77862, 77862, 77862, 77862, 77862, 89),
    (328239, 1079654, 2765367, 601216, 1159585, 857349, 74256, 1150082, 597252, 2362371, 79911, 79911, 79911, 79911, 79911, 79911, 79911, 79911, 79911, 76),
    (1853609, 2883744, 211594, 2242689, 790630, 2165293, 793926, 2169613, 598277, 2698274, 82948, 81960, 81960, 81960, 81960, 81960, 81960, 81960, 81960, 123),
    (1855848, 1661313, 66632, 2691458, 2098209, 268391, 2956359, 8294, 2766244, 2632101, 84009, 84009, 84009, 84009, 84009, 84009, 84009, 84009, 84009, 123),
    (740011, 1071234, 68937, 2955651, 794696, 2180260, 1058, 736288, 2369957, 2636801, 2109734, 86058, 86058, 86058, 86058, 86058, 86058, 86058, 86058, 125),
    (1073708, 792938, 2773252, 216484, 337922, 265507, 2894881, 147718, 2168137, 2176104, 65543, 2178048, 88107, 88107, 88107, 88107, 88107, 88107, 88107, 119),
    (743844, 339019, 2369898, 2236947, 621898, 6278, 2437417, 2168994, 2232359, 67912, 2099360, 2360585, 2704775, 90156, 90156, 90156, 90156, 90156, 90156, 119),
    (862316, 2239564, 204975, 799083, 2251878, 866467, 1153386, 328707, 68612, 2643079, 2097680, 5121, 84008, 2167816, 93193, 92205, 92205, 92205, 92205, 93),
    (1931382, 1603693, 2254982, 76343, 866412, 1092684, 2107956, 2898080, 2359952, 16484, 743985, 2175401, 2179107, 68683, 611331, 332339, 2379018, 2102273, 95236, 77),
    (606903, 618727, 2901447, 78390, 747945, 2109968, 2780169, 66097, 329765, 2125868, 2239488, 808204, 2183202, 3409956, 613572, 72706, 2104331, 96303, 96303, 238),
    (887095, 65864, 96401, 80009, 1117224, 873472, 210191, 5121, 2242894, 2110766, 2118060, 7714, 2646059, 2181133, 11309, 74763, 2106403, 99365, 98352, 119),
    (348833, 688232, 2244873, 877697, 2232482, 2384043, 2196491, 2117635, 2432041, 12295, 97318, 2367524, 29711, 2178350, 26661, 2108461, 100401, 100401, 100401, 119),
    (755882, 347402, 2116689, 557228, 2908264, 2244739, 2169133, 23600, 2386052, 2101282, 881700, 474155, 2172933, 2242607, 2109478, 2128910, 102450, 102450, 102450, 85),
    (874610, 2790731, 86188, 6257, 9356, 355409, 2911242, 1131684, 2169262, 273416, 2502694, 19598, 2173040, 621584, 2181159, 2112655, 104499, 104499, 104499, 85),
    (236012, 3317132, 354820, 2911268, 757765, 2185291, 2789806, 1388586, 2912369, 2436433, 358672, 80906, 2914537, 148486, 2247728, 2180103, 106548, 106548, 106548, 85),
    (762029, 2794957, 1388974, 221349, 2388997, 2792051, 96299, 295218, 2251846, 2391314, 100519, 86568, 2254097, 2118663, 2113577, 2116656, 108597, 108597, 108597, 85),
    (633006, 340247, 3321294, 1286448, 3440815, 2390029, 2269745, 1392679, 2373676, 1285393, 88585, 2110803, 2182152, 2122827, 87085, 2117682, 111634, 110646, 110646, 92),
    (227504, 569447, 1412752, 345167, 1209745, 568391, 2322569, 1134644, 2663560, 2206774, 103529, 628973, 2137101, 91282, 2122762, 2119723, 112695, 112695, 112695, 105),
    (492064, 2130105, 243865, 381480, 2197521, 2275506, 1127432, 18543, 177193, 87186, 2340362, 240719, 301134, 2201645, 2124846, 90635, 42027, 2204684, 115733, 51),
    (1116346, 114897, 2277554, 346224, 2130039, 2116754, 2117674, 2275475, 1334451, 2447983, 368684, 2122772, 306767, 2142262, 1141877, 2197518, 2192397, 116793, 116793, 51),
    (1118386, 2396281, 2279594, 231603, 2118737, 2398251, 3430488, 1278132, 2261036, 2400375, 306316, 1145879, 110765, 95373, 2143247, 2206734, 119864, 118842, 118842, 19),
    (250099, 2399322, 368683, 2119801, 2400428, 2279442, 232460, 2402357, 2132150, 1277976, 2385965, 95760, 113714, 2389142, 97464, 2145295, 120891, 120891, 120891, 17),
    (252084, 2400772, 371803, 90629, 2402355, 2252922, 26806, 2452570, 247986, 95251, 2134063, 2149526, 35982, 2328760, 2195472, 113688, 2407567, 122940, 122940, 17),
    (1058997, 255125, 373852, 354427, 2284557, 2404404, 97364, 94392, 2408506, 374803, 1073202, 2282647, 2202639, 117778, 2125841, 1147953, 2149392, 124989, 124989, 17),
    (256550, 94390, 240733, 96440, 255126, 310424, 2391095, 2388025, 2285691, 361493, 2138228, 119961, 2131035, 35378, 39985, 2282514, 128051, 127038, 127038, 17),
    (377383, 178238, 2158703, 2129048, 126007, 176176, 2156729, 382105, 1289846, 35506, 2129980, 2199186, 121877, 38996, 2202652, 2204699, 130074, 129087, 129087, 0),
)
EVENTS = 2 * (len(PLAN[0]) - 1)
ROWS = 256
BLOCK = 512
INFO = 16
SLOT = 2 * ROWS + INFO


def pick(values, index):
    result = jnp.int32(values[0])
    for at in range(1, len(values)):
        result = jnp.where(index == at, jnp.int32(values[at]), result)
    return result


def kernel(
    x_hbm, gain_hbm, wqkv_hbm, wout_hbm, seg_hbm, out_ref,
    xbuf, gain_ref, wqkv, wcol, seg_ref, kv, give, qgive, qrows, qmask, acc, run_max, run_sum, ogive, att,
    local_sem, x_send, x_recv, w_send, w_recv, s_send, s_recv, kv_send, kv_recv, o_send, o_recv,
):
    f32, bf16 = jnp.float32, jnp.bfloat16
    seq, head = lax.axis_index("seq"), lax.axis_index("head")
    core = lax.rem(seq, 2)
    chip = lax.div(seq, 2)
    z = lax.rem(chip, 8)
    x = lax.div(chip, 8)
    other = 1 - core

    def at(xx, zz, cc):
        return (xx * 8 + zz) * 2 + cc

    z_up, z_down = lax.rem(z + 1, 8), lax.rem(z + 7, 8)
    x_up, x_down = lax.rem(x + 1, 4), lax.rem(x + 3, 4)
    up = (at(x, z_up, core), head)
    down = (at(x, z_down, core), head)
    right = (at(x_up, z, core), head)
    left = (at(x_down, z, core), head)
    partner = (at(x, z, other), head)
    y_of = [lax.rem(head + j, 4) for j in range(4)]

    barrier = pltpu.get_barrier_semaphore()
    greeted = [up, down, right, left, partner]
    for j in range(1, 4):
        greeted.append((seq, y_of[j]))
        greeted.append((at(x, z, other), y_of[j]))
    for device in greeted:
        pl.semaphore_signal(barrier, inc=1, device_id=device, device_id_type=MESH)

    seg_in = pltpu.make_async_copy(seg_hbm, seg_ref, local_sem.at[3])
    seg_in.start()
    gain_in = pltpu.make_async_copy(gain_hbm, gain_ref, local_sem.at[4])
    gain_in.start()
    mine = pltpu.make_async_copy(x_hbm, xbuf.at[head], local_sem.at[0])
    mine.start()
    weights_in = pltpu.make_async_copy(wqkv_hbm, wqkv, local_sem.at[1])
    weights_in.start()
    columns = pl.ds(pl.multiple_of(head * ROWS, ROWS), ROWS)
    wcol_in = pltpu.make_async_copy(wout_hbm.at[:, columns], wcol.at[head], local_sem.at[2])
    wcol_in.start()

    pl.semaphore_wait(barrier, len(greeted))

    x_copies = []
    for j in (2, 1, 3):
        copy = pltpu.make_async_remote_copy(
            src_ref=x_hbm, dst_ref=xbuf.at[head], send_sem=x_send.at[j], recv_sem=x_recv.at[head],
            device_id=(seq, y_of[j]), device_id_type=MESH)
        copy.start()
        x_copies.append(copy)
    seg_in.wait()
    seg = seg_ref[...]
    lane = lax.broadcasted_iota(jnp.int32, (1, HD), 1)
    sub = lax.broadcasted_iota(jnp.int32, (INFO, HD), 0)
    lower = jnp.zeros((1, HD), f32)
    upper = jnp.zeros((1, HD), f32)
    for t in range(1, 5):
        before = jnp.sum(jnp.where(seg < t, 1.0, 0.0).astype(f32), axis=1, keepdims=True)
        before = before[0:1] + before[1:2]
        lower = jnp.where(lane == t, before, lower)
        upper = jnp.where(lane == t - 1, before, upper)
    lower = jnp.where(lane < 4, lower, 0.0)
    info = jnp.where(sub == 0, lower, jnp.where(sub == 1, upper, 0.0)).astype(bf16)

    mine_at = core * 32 + chip
    words = [pick([row[i] for row in PLAN], mine_at) for i in range(len(PLAN[0]))]
    gain_in.wait()
    mine.wait()
    weights_in.wait()
    wcol_in.wait()
    for j in range(1, 4):
        pltpu.make_async_remote_copy(
            src_ref=x_hbm, dst_ref=xbuf.at[y_of[j]], send_sem=x_send.at[j], recv_sem=x_recv.at[y_of[j]],
            device_id=(seq, y_of[j]), device_id_type=MESH).wait_recv()

    w_copies = []
    for j in range(1, 4):
        theirs = pl.ds(pl.multiple_of(y_of[j] * ROWS, ROWS), ROWS)
        copy = pltpu.make_async_remote_copy(
            src_ref=wout_hbm.at[:, theirs], dst_ref=wcol.at[head], send_sem=w_send.at[j],
            recv_sem=w_recv.at[head], device_id=(seq, y_of[j]), device_id_type=MESH)
        copy.start()
        w_copies.append(copy)

    parts = [xbuf[y].astype(f32) for y in range(4)]
    squares = sum(jnp.sum(part * part, axis=1, keepdims=True) for part in parts)
    scale = lax.rsqrt(squares * (1.0 / 1024.0) + epsilon)
    normed = jnp.concatenate(
        [(parts[y] * scale * gain_ref[:, y * ROWS : (y + 1) * ROWS]).astype(bf16) for y in range(4)], axis=1)

    def project(which):
        return jnp.dot(normed, wqkv[which], preferred_element_type=f32)

    def hand_on(direction, piece):
        device = (up, down, right, left)[direction]
        return pltpu.make_async_remote_copy(
            src_ref=kv.at[piece], dst_ref=kv.at[piece], send_sem=kv_send.at[direction, piece],
            recv_sem=kv_recv.at[piece], device_id=device, device_id_type=MESH)

    own = pl.ds(pl.multiple_of(core * ROWS, ROWS), ROWS)
    own_piece = core * 32 + chip
    other_piece = other * 32 + chip

    def swap(j, source, target, landing):
        return pltpu.make_async_remote_copy(
            src_ref=source, dst_ref=target, send_sem=s_send.at[j], recv_sem=landing,
            device_id=partner, device_id_type=MESH)

    give[2 * ROWS : SLOT, :] = info
    kv[own_piece, 2 * ROWS : SLOT, :] = info
    for j in (1, 2):
        both = project(j).astype(bf16)
        first, second = both[:, :HD], both[:, HD:]
        give[(j - 1) * ROWS : j * ROWS, :] = jnp.where(core == 0, second, first)
        kv[own_piece, (j - 1) * ROWS : j * ROWS, :] = jnp.where(core == 0, first, second)

    own_flag = [lax.rem(lax.div(words[-1], 1 << i), 2) == 1 for i in range(8)]
    s_copies = [swap(0, give, kv.at[own_piece], kv_recv.at[own_piece])]
    s_copies[0].start()
    for direction in range(4):
        @pl.when(own_flag[direction])
        def _(direction=direction):
            hand_on(direction, own_piece).start()

    both = (project(0) * (1.0 / math.sqrt(HD))).astype(bf16)
    first, second = both[:, :HD], both[:, HD:]
    qgive[...] = jnp.where(core == 0, second, first)
    s_copies.append(swap(1, qgive, qrows.at[own], s_recv.at[1]))
    s_copies[1].start()
    qrows[own, :] = jnp.where(core == 0, first, second)

    swap(0, give, kv.at[other_piece], kv_recv.at[other_piece]).wait_recv()
    for direction in range(4):
        @pl.when(own_flag[4 + direction])
        def _(direction=direction):
            hand_on(direction, other_piece).start()
    s_copies[1].wait_recv()

    def event(e):
        pair = lax.div(e, 2)
        word = words[0]
        for i in range(1, len(words) - 1):
            word = jnp.where(pair == i, words[i], word)
        code = jnp.where(lax.rem(e, 2) == 0, lax.rem(word, 2048), lax.div(word, 2048))
        piece = lax.rem(code, 64)
        flag = [lax.rem(lax.div(code, 64 << i), 2) == 1 for i in range(5)]
        source = lax.rem(piece, 32)
        return source != chip, piece, source, flag

    row = lax.broadcasted_iota(jnp.int32, (ROWS, HD), 0).astype(f32)
    lanes = lax.broadcasted_iota(jnp.int32, (ROWS, HD), 1)

    def inside(piece):
        bounds = kv[piece, 2 * ROWS : SLOT, :].astype(f32)
        return (row >= bounds[0:1, :]) & (row < bounds[1:2, :])

    for half in range(2):
        qmask[half * ROWS : (half + 1) * ROWS, :] = jnp.where(
            inside(half * 32 + chip) | (lanes >= 4), 0.0, masked_score).astype(bf16)

    def keys_of(piece):
        return jnp.concatenate(
            [kv[piece, 0:ROWS, :], jnp.where(inside(piece), 1.0, 0.0).astype(bf16)], axis=1)

    def scores_of(part, keys):
        rows = slice(part * ROWS, (part + 1) * ROWS)
        queries = jnp.concatenate([qrows[rows, :], qmask[rows, :]], axis=1)
        return lax.dot_general(queries, keys, (((1,), (1,)), ((), ())), preferred_element_type=f32)

    def keep(part, new_max, total, product):
        rows = slice(part * ROWS, (part + 1) * ROWS)
        run_max[rows, :] = jnp.broadcast_to(new_max, (ROWS, HD))
        run_sum[rows, :] = jnp.broadcast_to(total, (ROWS, HD))
        acc[rows, :] = product

    own_keys = [keys_of(chip), keys_of(32 + chip)]
    own_values = [kv[half * 32 + chip, ROWS : 2 * ROWS, :] for half in range(2)]
    q_at = lax.broadcasted_iota(jnp.int32, (ROWS, ROWS), 0)
    k_at = lax.broadcasted_iota(jnp.int32, (ROWS, ROWS), 1)
    for part in range(2):
        scores = [scores_of(part, own_keys[half]) for half in range(part + 1)]
        scores[part] = jnp.where(k_at <= q_at, scores[part], masked_score)
        new_max = jnp.max(scores[part], axis=1, keepdims=True)
        if part == 1:
            new_max = jnp.maximum(new_max, jnp.max(scores[0], axis=1, keepdims=True))
        total, product = 0.0, 0.0
        for half in range(part + 1):
            weights = jnp.exp(scores[half] - new_max)
            total = total + jnp.sum(weights, axis=1, keepdims=True)
            product = product + jnp.dot(
                weights.astype(bf16), own_values[half], preferred_element_type=f32)
        keep(part, new_max, total, product)

    def attend(source):
        keys = jnp.concatenate([keys_of(source), keys_of(32 + source)], axis=0)
        values = jnp.concatenate(
            [kv[half * 32 + source, ROWS : 2 * ROWS, :] for half in range(2)], axis=0)
        queries = jnp.concatenate([qrows[...], qmask[...]], axis=1)
        scores = lax.dot_general(
            queries, keys, (((1,), (1,)), ((), ())), preferred_element_type=f32)
        old_max = run_max[...]
        new_max = jnp.maximum(old_max, jnp.max(scores, axis=1, keepdims=True))
        weights = jnp.exp(scores - jnp.concatenate([new_max] * (BLOCK // HD), axis=1))
        factor = jnp.exp(old_max - new_max)
        run_max[...] = new_max
        run_sum[...] = run_sum[...] * factor + jnp.sum(weights, axis=1, keepdims=True)
        acc[...] = acc[...] * factor + jnp.dot(
            weights.astype(bf16), values, preferred_element_type=f32)

    def step(e, carry):
        valid, piece, source, flag = event(e)

        @pl.when(valid)
        def _():
            hand_on(0, piece).wait_recv()
            for direction in range(4):
                @pl.when(flag[direction])
                def _(direction=direction):
                    hand_on(direction, piece).start()

            @pl.when(flag[4])
            def _():
                attend(source)

        return carry

    lax.fori_loop(0, EVENTS, step, 0)

    for half in range(2):
        rows = slice(half * ROWS, (half + 1) * ROWS)
        ogive[half] = (acc[rows, :] / run_sum[rows, 0:1]).astype(bf16)

    o_copies = []
    lot = head * 2 + core
    for j in (2, 1, 3, 0):
        for c in range(2):
            if j == 0 and c == 0:
                continue
            row_core = core if c == 0 else other
            copy = pltpu.make_async_remote_copy(
                src_ref=ogive.at[row_core], dst_ref=att.at[lot], send_sem=o_send.at[j * 2 + c],
                recv_sem=o_recv.at[lot], device_id=(at(x, z, row_core), y_of[j]), device_id_type=MESH)
            copy.start()
            o_copies.append(copy)
    att[lot] = ogive[core]

    for direction in range(8):
        @pl.when(own_flag[direction])
        def _(direction=direction):
            hand_on(direction % 4, own_piece if direction < 4 else other_piece).wait_send()

    def drain(e, carry):
        valid, piece, source, flag = event(e)
        for direction in range(4):
            @pl.when(flag[direction])
            def _(direction=direction):
                hand_on(direction, piece).wait_send()
        return carry

    lax.fori_loop(0, EVENTS, drain, 0)
    for copy in x_copies + w_copies + s_copies:
        copy.wait_send()

    for j in range(1, 4):
        pltpu.make_async_remote_copy(
            src_ref=wout_hbm.at[:, columns], dst_ref=wcol.at[y_of[j]], send_sem=w_send.at[j],
            recv_sem=w_recv.at[y_of[j]], device_id=(seq, y_of[j]), device_id_type=MESH).wait_recv()
    total = None
    for j in (0, 1, 3, 2):
        for c in range(2):
            if j == 0 and c == 0:
                continue
            lot_of = y_of[j] * 2 + (core if c == 0 else other)
            pltpu.make_async_remote_copy(
                src_ref=ogive.at[core], dst_ref=att.at[lot_of], send_sem=o_send.at[j * 2 + c],
                recv_sem=o_recv.at[lot_of], device_id=partner, device_id_type=MESH).wait_recv()
        both = jnp.concatenate([att[2 * y_of[j]], att[2 * y_of[j] + 1]], axis=1)
        term = jnp.dot(both, wcol[y_of[j]], preferred_element_type=f32)
        total = term if total is None else total + term
    out_ref[...] = total.astype(bf16)

    for copy in o_copies:
        copy.wait_send()


def per_device(face_rows, norm_gain, w_qkv, w_out, segments):
    bf16, f32 = jnp.bfloat16, jnp.float32
    vmem = pl.BlockSpec(memory_space=pltpu.VMEM)
    hbm = pl.BlockSpec(memory_space=pl.ANY)
    dma = pltpu.SemaphoreType.DMA
    return pl.pallas_call(
        kernel,
        name="face_attention",
        out_shape=jax.ShapeDtypeStruct((ROWS, ROWS), bf16),
        in_specs=[hbm, hbm, hbm, hbm, hbm],
        out_specs=vmem,
        scratch_shapes=[
            pltpu.VMEM((4, ROWS, ROWS), bf16),
            pltpu.VMEM((1, 1024), f32),
            pltpu.VMEM((3, 1024, ROWS), bf16),
            pltpu.VMEM((4, ROWS, ROWS), bf16),
            pltpu.VMEM((2, HD), jnp.int32),
            pltpu.VMEM((64, SLOT, HD), bf16),
            pltpu.VMEM((SLOT, HD), bf16),
            pltpu.VMEM((ROWS, HD), bf16),
            pltpu.VMEM((BLOCK, HD), bf16),
            pltpu.VMEM((BLOCK, HD), bf16),
            pltpu.VMEM((BLOCK, HD), f32),
            pltpu.VMEM((BLOCK, HD), f32),
            pltpu.VMEM((BLOCK, HD), f32),
            pltpu.VMEM((2, ROWS, HD), bf16),
            pltpu.VMEM((8, ROWS, HD), bf16),
            dma((5,)),
            dma((4,)), dma((4,)),
            dma((4,)), dma((4,)),
            dma((4,)), dma((4,)),
            dma((4, 64)), dma((64,)),
            dma((8,)), dma((8,)),
        ],
        compiler_params=pltpu.CompilerParams(
            collective_id=0, has_side_effects=True, vmem_limit_bytes=67043328),
    )(
        face_rows,
        norm_gain.reshape(1, 1024),
        jnp.transpose(w_qkv, (1, 0, 2)),
        w_out,
        segments.reshape(2, HD),
    )


def solution(mesh):
    in_specs = (P("seq", "head"), P(), P(None, None, "head"), P("head", None), P("seq"))
    out_specs = P("seq", "head")
    return jax.shard_map(
        per_device, mesh=mesh, in_specs=in_specs, out_specs=out_specs, check_vma=False
    )
```

```python
import functools
import math

import jax
import jax.numpy as jnp
from jax import lax
from jax.experimental import pallas as pl
from jax.experimental.pallas import tpu as pltpu
from jax.sharding import PartitionSpec as P

MESH = pl.DeviceIdType.MESH
HD = 128
epsilon = 1e-05
masked_score = -1e30
PLAN = (
    (1067425, 1651074, 539177, 1073570, 1141292, 0, 0, 0, 0, 0, 0, 0, 0, 0, 0, 0, 0, 0, 0, 255),
    (1067328, 1394818, 1070176, 1065378, 1336107, 2732, 2049, 2049, 2049, 2049, 2049, 2049, 2049, 2049, 2049, 2049, 2049, 2049, 2049, 117),
    (2296129, 532771, 2818112, 1335979, 1141420, 4098, 4098, 4098, 4098, 4098, 4098, 4098, 4098, 4098, 4098, 4098, 4098, 4098, 4098, 255),
    (135556, 1402210, 1141029, 65857, 1152353, 7168, 6147, 6147, 6147, 6147, 6147, 6147, 6147, 6147, 6147, 6147, 6147, 6147, 6147, 53),
    (1073413, 862531, 2824748, 1087490, 1144162, 2296129, 1151232, 9504, 8196, 8196, 8196, 8196, 8196, 8196, 8196, 8196, 8196, 8196, 8196, 91),
    (537101, 1091908, 540004, 137902, 2824320, 2949154, 2165057, 11266, 10245, 10245, 10245, 10245, 10245, 10245, 10245, 10245, 10245, 10245, 10245, 191),
    (1077895, 2828357, 729472, 2950468, 661890, 2824720, 1087489, 2165794, 12294, 12294, 12294, 12294, 12294, 12294, 12294, 12294, 12294, 12294, 12294, 83),
    (537103, 1144960, 2950246, 67845, 267301, 2429037, 2099492, 7428, 15651, 14343, 14343, 14343, 14343, 14343, 14343, 14343, 14343, 14343, 14343, 74),
    (649, 2294185, 211329, 791969, 2765030, 530757, 2112674, 351523, 140645, 17700, 16392, 16392, 16392, 16392, 16392, 16392, 16392, 16392, 16392, 117),
    (789002, 2835016, 131362, 269665, 735403, 210339, 861254, 2243616, 2173253, 2106370, 18441, 18441, 18441, 18441, 18441, 18441, 18441, 18441, 18441, 251),
    (397641, 2312747, 2167308, 672131, 2834433, 1666531, 2957572, 2228320, 212001, 2633766, 535559, 21541, 20490, 20490, 20490, 20490, 20490, 20490, 20490, 87),
    (151692, 1139075, 9578, 1402953, 71076, 2232882, 2172933, 148841, 537640, 3363, 2295840, 2700288, 2701575, 22539, 22539, 22539, 22539, 22539, 22539, 117),
    (878923, 2840740, 1087877, 151619, 2173956, 2314374, 674851, 201266, 2102694, 2701447, 3113, 2179080, 2164736, 25632, 24588, 24588, 24588, 24588, 24588, 255),
    (680469, 1667077, 930924, 677892, 2317348, 802214, 2963459, 2169162, 345125, 1130, 2181129, 70688, 2113601, 2165762, 26637, 26637, 26637, 26637, 26637, 61),
    (2845005, 342182, 207180, 869740, 393744, 543750, 74759, 154793, 2106376, 2107923, 152875, 1378434, 138272, 2168106, 2100259, 28686, 28686, 28686, 28686, 109),
    (997390, 280744, 143629, 2444295, 3762208, 1051656, 549061, 2192545, 2176101, 75052, 2097154, 2237602, 20491, 2710570, 2168835, 30735, 30735, 30735, 30735, 204),
    (886920, 1320, 2324559, 282793, 2119, 2115918, 2178081, 2164138, 2715915, 682022, 2240514, 2190370, 137221, 2187276, 2173987, 9259, 33828, 32784, 32784, 87),
    (215120, 2326666, 2969601, 5129, 809000, 2447439, 2429999, 1195016, 554017, 2308268, 2121830, 92195, 74765, 2110596, 2172933, 2192387, 34833, 34833, 34833, 117),
    (166346, 2969907, 266379, 2448497, 688201, 2182178, 16387, 353648, 556136, 2122787, 2451469, 14532, 2170894, 2177701, 79022, 2194438, 37893, 36882, 36882, 85),
    (692619, 3380651, 6412, 2449482, 167018, 206129, 18573, 338318, 164969, 2327597, 2453510, 2168872, 2176005, 97284, 2127943, 2178056, 38931, 38931, 38931, 117),
    (286997, 2581075, 1057907, 813067, 3379538, 2976142, 2316325, 2453514, 2315397, 165897, 78255, 2391076, 2313222, 278567, 2719760, 2112561, 42024, 40980, 40980, 85),
    (289108, 10550, 816500, 2453587, 91685, 359795, 153798, 2128908, 692872, 2200678, 623917, 101419, 2177031, 87312, 2442321, 2115625, 44042, 43029, 43029, 91),
    (698574, 2323765, 172688, 1062925, 2859439, 1219757, 25224, 2178063, 2458668, 2857137, 85224, 2508806, 153610, 37931, 2176042, 2133042, 45078, 45078, 45078, 52),
    (162192, 2586934, 1327623, 2570318, 362773, 3372054, 2195533, 2320553, 282644, 25908, 3232821, 2132243, 37939, 2180140, 23730, 2186249, 47127, 47127, 47127, 68),
    (164352, 1114265, 380144, 363271, 2394199, 1067087, 2340904, 1257618, 177263, 2181130, 2338830, 2114738, 2183221, 38923, 2271756, 2188398, 27827, 2189332, 2186292, 51),
    (428120, 1067154, 2329720, 33833, 2461834, 1328176, 178323, 31786, 2342067, 2447435, 1073702, 42095, 177196, 29748, 93302, 2191381, 2124853, 51225, 51225, 51),
    (1052818, 1118297, 2346162, 301066, 2463768, 2183249, 88144, 2343060, 2198028, 2466860, 2326615, 43181, 31863, 3374091, 177333, 2386998, 2191374, 53274, 53274, 17),
    (301146, 2333818, 182420, 2465803, 2345004, 1124370, 306219, 2199633, 2467885, 2121784, 2328630, 291981, 2453527, 2195536, 2147383, 2127919, 56342, 55323, 55323, 17),
    (1056916, 2465883, 1387643, 305164, 2467930, 2348076, 288790, 2469939, 2267288, 356370, 47193, 1342478, 2210937, 35885, 2331704, 3247215, 2195472, 57372, 57372, 17),
    (188933, 371365, 2351117, 172182, 2469979, 2204693, 2349208, 2125934, 184471, 2472591, 105594, 2137272, 36953, 101433, 99373, 2133042, 2194448, 59421, 59421, 17),
    (438365, 2353671, 311310, 188437, 2351255, 2337423, 2472020, 187576, 2193968, 2208891, 2192436, 184377, 2348048, 2394289, 36915, 2149426, 62483, 61470, 61470, 17),
    (311879, 440350, 2603215, 2475070, 2324509, 1224729, 3506192, 2602045, 58553, 363580, 2271861, 3442772, 1347611, 2335803, 54962, 39994, 64563, 63519, 63519, 0),
    (670248, 1312929, 1380872, 1135153, 1141262, 1075493, 65568, 65568, 65568, 65568, 65568, 65568, 65568, 65568, 65568, 65568, 65568, 65568, 65568, 230),
    (332034, 596530, 66218, 1073223, 2228747, 67617, 67617, 67617, 67617, 67617, 67617, 67617, 67617, 67617, 67617, 67617, 67617, 67617, 67617, 119),
    (199338, 530851, 2230827, 539275, 1141388, 2163008, 69666, 69666, 69666, 69666, 69666, 69666, 69666, 69666, 69666, 69666, 69666, 69666, 69666, 247),
    (1333803, 1057122, 2756748, 723629, 1217857, 328207, 72704, 71715, 71715, 71715, 71715, 71715, 71715, 71715, 71715, 71715, 71715, 71715, 71715, 127),
    (203308, 1336643, 201478, 2757166, 852257, 1342465, 1086464, 73764, 73764, 73764, 73764, 73764, 73764, 73764, 73764, 73764, 73764, 73764, 73764, 117),
    (274532, 2761229, 203438, 2759072, 70287, 1090944, 2626099, 1146881, 76833, 75813, 75813, 75813, 75813, 75813, 75813, 75813, 75813, 75813, 75813, 85),
    (356453, 1145095, 853829, 2359396, 1079831, 68932, 728193, 70723, 1090064, 2626098, 77862, 77862, 77862, 77862, 77862, 77862, 77862, 77862, 77862, 101),
    (602272, 732544, 1208737, 2633089, 1094198, 2109476, 2629794, 530509, 2169986, 79911, 79911, 79911, 79911, 79911, 79911, 79911, 79911, 79911, 79911, 116),
    (555488, 211081, 2228785, 734279, 1272194, 2765858, 858145, 207140, 2100227, 2237765, 82091, 81960, 81960, 81960, 81960, 81960, 81960, 81960, 81960, 255),
    (723048, 2245170, 1246465, 856423, 334978, 337408, 2891015, 616550, 2109797, 2106629, 84009, 84009, 84009, 84009, 84009, 84009, 84009, 84009, 84009, 116),
    (332587, 737609, 2101283, 2365604, 3336, 196615, 13607, 2229252, 2164741, 2176041, 87077, 86058, 86058, 86058, 86058, 86058, 86058, 86058, 86058, 89),
    (203114, 337155, 1142090, 149602, 2101778, 67973, 737574, 2493477, 2897028, 80937, 2635808, 2114560, 88107, 88107, 88107, 88107, 88107, 88107, 88107, 155),
    (354788, 2775339, 797956, 217510, 2249893, 2371683, 2103719, 2898018, 555017, 67616, 83009, 2098568, 2182146, 90156, 90156, 90156, 90156, 90156, 90156, 157),
    (862510, 2369900, 2777510, 2110351, 1089636, 867332, 1153355, 65576, 2898026, 1146883, 2376832, 2317642, 2168834, 1116169, 2100322, 93481, 92205, 92205, 92205, 215),
    (340783, 1866093, 867782, 345165, 1097095, 10348, 2901068, 204832, 2097680, 1090564, 280843, 329763, 1151274, 2100261, 2444298, 201771, 2102275, 94254, 94254, 95),
    (868839, 3174702, 1160455, 223334, 1094792, 263750, 3697033, 338081, 2163905, 615493, 1052740, 21772, 2168963, 2182180, 2166827, 2184203, 96303, 96303, 96303, 54),
    (213681, 2507186, 65961, 2115951, 300495, 2087, 2098721, 209262, 135562, 2241543, 203435, 615458, 2445357, 2104397, 2256932, 11531, 2106636, 99365, 98352, 119),
    (1002162, 230793, 2785426, 329768, 752010, 2100232, 2783330, 350247, 2183596, 77955, 2382919, 225316, 2102404, 2169862, 2121837, 2107621, 2126861, 100401, 100401, 87),
    (807281, 72785, 350636, 3360841, 622632, 2383184, 335874, 2167151, 552068, 2122824, 29775, 77863, 2112558, 11270, 2190373, 2104362, 102450, 102450, 102450, 115),
    (565618, 876579, 480850, 335883, 232491, 2788483, 3417162, 1264013, 2189445, 558348, 2173094, 96398, 2719784, 2247726, 2371623, 2128904, 105479, 104499, 104499, 85),
    (759980, 2791701, 92324, 219506, 2266253, 338955, 217486, 2384900, 143792, 2107697, 2191407, 2264336, 343078, 82954, 1133575, 2114575, 107529, 106548, 106548, 117),
    (762029, 3318925, 1284142, 2912421, 2267824, 882796, 208946, 1269136, 345164, 2129234, 86321, 2109479, 2108427, 2112529, 19466, 2182152, 108597, 108597, 108597, 117),
    (239918, 2912791, 886101, 762031, 3319440, 344173, 760847, 2791857, 90118, 80434, 1133606, 273415, 2377771, 21640, 2133004, 2124875, 2184210, 110646, 110646, 85),
    (752048, 2916918, 345622, 211121, 225714, 2730261, 1395720, 2242868, 2378770, 1331309, 2129101, 2662444, 2252843, 3232019, 2133006, 3169331, 112695, 112695, 112695, 100),
    (378992, 1049089, 243866, 2459793, 241817, 18578, 225826, 82474, 2117811, 2114647, 3175474, 2273423, 2182163, 2129963, 108557, 2194453, 91181, 2119700, 2122804, 51),
    (245809, 2277530, 99537, 280722, 367632, 21554, 350327, 97834, 369811, 91215, 3170357, 2119734, 225325, 2182231, 2143253, 2126861, 117780, 116793, 116793, 51),
    (299129, 1120770, 87129, 231603, 245931, 2118803, 2278923, 2132148, 91186, 370736, 245260, 2401296, 227501, 111765, 2386959, 2191502, 2143255, 118842, 118842, 49),
    (250531, 1136819, 2399322, 370187, 248324, 370866, 2280596, 90161, 246381, 2264213, 373848, 2135053, 2388526, 30775, 2122799, 2195472, 2405399, 120891, 120891, 17),
    (368763, 371803, 91156, 249907, 27797, 2283020, 1061907, 247990, 234158, 2389081, 99437, 245775, 2132017, 310290, 2147344, 2405423, 123959, 122940, 122940, 17),
    (289013, 186550, 253966, 2140211, 2285588, 2191511, 358416, 103547, 2405428, 2127994, 2195505, 52250, 2346066, 50359, 2133011, 2190392, 124989, 124989, 124989, 17),
    (309430, 2404476, 311813, 96277, 2472027, 302133, 2127886, 107153, 2139182, 2285661, 2350205, 2201616, 249874, 2196536, 117809, 2151449, 128050, 127038, 127038, 17),
    (1077495, 2275390, 241816, 1346646, 174137, 2337945, 2198712, 2269236, 122931, 32922, 2195506, 2159635, 97308, 2134043, 60475, 2128957, 130106, 129087, 129087, 0),
)
EVENTS = 2 * (len(PLAN[0]) - 1)
ROWS = 256
BLOCK = 512
INFO = 16
SLOT = 2 * ROWS + INFO


def pick(values, index):
    result = jnp.int32(values[0])
    for at in range(1, len(values)):
        result = jnp.where(index == at, jnp.int32(values[at]), result)
    return result


def kernel(
    x_hbm, gain_hbm, wqkv_hbm, wout_hbm, seg_hbm, out_ref,
    xbuf, gain_ref, wqkv, wcol, seg_ref, kv, give, qgive, qrows, qmask, acc, run_max, run_sum, ogive, att,
    local_sem, x_send, x_recv, w_send, w_recv, s_send, s_recv, kv_send, kv_recv, o_send, o_recv,
):
    f32, bf16 = jnp.float32, jnp.bfloat16
    seq, head = lax.axis_index("seq"), lax.axis_index("head")
    core = lax.rem(seq, 2)
    chip = lax.div(seq, 2)
    z = lax.rem(chip, 8)
    x = lax.div(chip, 8)
    other = 1 - core

    def at(xx, zz, cc):
        return (xx * 8 + zz) * 2 + cc

    z_up, z_down = lax.rem(z + 1, 8), lax.rem(z + 7, 8)
    x_up, x_down = lax.rem(x + 1, 4), lax.rem(x + 3, 4)
    up = (at(x, z_up, core), head)
    down = (at(x, z_down, core), head)
    right = (at(x_up, z, core), head)
    left = (at(x_down, z, core), head)
    partner = (at(x, z, other), head)
    y_of = [lax.rem(head + j, 4) for j in range(4)]

    barrier = pltpu.get_barrier_semaphore()
    greeted = [up, down, right, left, partner]
    for j in range(1, 4):
        greeted.append((seq, y_of[j]))
        greeted.append((at(x, z, other), y_of[j]))
    for device in greeted:
        pl.semaphore_signal(barrier, inc=1, device_id=device, device_id_type=MESH)

    seg_in = pltpu.make_async_copy(seg_hbm, seg_ref, local_sem.at[3])
    seg_in.start()
    gain_in = pltpu.make_async_copy(gain_hbm, gain_ref, local_sem.at[4])
    gain_in.start()
    mine = pltpu.make_async_copy(x_hbm, xbuf.at[head], local_sem.at[0])
    mine.start()
    weights_in = pltpu.make_async_copy(wqkv_hbm, wqkv, local_sem.at[1])
    weights_in.start()
    columns = pl.ds(pl.multiple_of(head * ROWS, ROWS), ROWS)
    wcol_in = pltpu.make_async_copy(wout_hbm.at[:, columns], wcol.at[head], local_sem.at[2])
    wcol_in.start()

    pl.semaphore_wait(barrier, len(greeted))

    x_copies = []
    for j in (2, 1, 3):
        copy = pltpu.make_async_remote_copy(
            src_ref=x_hbm, dst_ref=xbuf.at[head], send_sem=x_send.at[j], recv_sem=x_recv.at[head],
            device_id=(seq, y_of[j]), device_id_type=MESH)
        copy.start()
        x_copies.append(copy)
    seg_in.wait()
    seg = seg_ref[...]
    lane = lax.broadcasted_iota(jnp.int32, (1, HD), 1)
    sub = lax.broadcasted_iota(jnp.int32, (INFO, HD), 0)
    lower = jnp.zeros((1, HD), f32)
    upper = jnp.zeros((1, HD), f32)
    for t in range(1, 5):
        before = jnp.sum(jnp.where(seg < t, 1.0, 0.0).astype(f32), axis=1, keepdims=True)
        before = before[0:1] + before[1:2]
        lower = jnp.where(lane == t, before, lower)
        upper = jnp.where(lane == t - 1, before, upper)
    lower = jnp.where(lane < 4, lower, 0.0)
    info = jnp.where(sub == 0, lower, jnp.where(sub == 1, upper, 0.0)).astype(bf16)

    mine_at = core * 32 + chip
    words = [pick([row[i] for row in PLAN], mine_at) for i in range(len(PLAN[0]))]
    gain_in.wait()
    mine.wait()
    weights_in.wait()
    wcol_in.wait()
    for j in range(1, 4):
        pltpu.make_async_remote_copy(
            src_ref=x_hbm, dst_ref=xbuf.at[y_of[j]], send_sem=x_send.at[j], recv_sem=x_recv.at[y_of[j]],
            device_id=(seq, y_of[j]), device_id_type=MESH).wait_recv()

    w_copies = []
    for j in range(1, 4):
        theirs = pl.ds(pl.multiple_of(y_of[j] * ROWS, ROWS), ROWS)
        copy = pltpu.make_async_remote_copy(
            src_ref=wout_hbm.at[:, theirs], dst_ref=wcol.at[head], send_sem=w_send.at[j],
            recv_sem=w_recv.at[head], device_id=(seq, y_of[j]), device_id_type=MESH)
        copy.start()
        w_copies.append(copy)

    parts = [xbuf[y].astype(f32) for y in range(4)]
    squares = sum(jnp.sum(part * part, axis=1, keepdims=True) for part in parts)
    scale = lax.rsqrt(squares * (1.0 / 1024.0) + epsilon)
    normed = jnp.concatenate(
        [(parts[y] * scale * gain_ref[:, y * ROWS : (y + 1) * ROWS]).astype(bf16) for y in range(4)], axis=1)

    def project(which):
        return jnp.dot(normed, wqkv[which], preferred_element_type=f32)

    def hand_on(direction, piece):
        device = (up, down, right, left)[direction]
        return pltpu.make_async_remote_copy(
            src_ref=kv.at[piece], dst_ref=kv.at[piece], send_sem=kv_send.at[direction, piece],
            recv_sem=kv_recv.at[piece], device_id=device, device_id_type=MESH)

    own = pl.ds(pl.multiple_of(core * ROWS, ROWS), ROWS)
    own_piece = core * 32 + chip
    other_piece = other * 32 + chip

    def swap(j, source, target, landing):
        return pltpu.make_async_remote_copy(
            src_ref=source, dst_ref=target, send_sem=s_send.at[j], recv_sem=landing,
            device_id=partner, device_id_type=MESH)

    give[2 * ROWS : SLOT, :] = info
    kv[own_piece, 2 * ROWS : SLOT, :] = info
    for j in (1, 2):
        both = project(j).astype(bf16)
        first, second = both[:, :HD], both[:, HD:]
        give[(j - 1) * ROWS : j * ROWS, :] = jnp.where(core == 0, second, first)
        kv[own_piece, (j - 1) * ROWS : j * ROWS, :] = jnp.where(core == 0, first, second)

    own_flag = [lax.rem(lax.div(words[-1], 1 << i), 2) == 1 for i in range(8)]
    s_copies = [swap(0, give, kv.at[own_piece], kv_recv.at[own_piece])]
    s_copies[0].start()
    for direction in range(4):
        @pl.when(own_flag[direction])
        def _(direction=direction):
            hand_on(direction, own_piece).start()

    both = (project(0) * (1.0 / math.sqrt(HD))).astype(bf16)
    first, second = both[:, :HD], both[:, HD:]
    qgive[...] = jnp.where(core == 0, second, first)
    s_copies.append(swap(1, qgive, qrows.at[own], s_recv.at[1]))
    s_copies[1].start()
    qrows[own, :] = jnp.where(core == 0, first, second)

    swap(0, give, kv.at[other_piece], kv_recv.at[other_piece]).wait_recv()
    for direction in range(4):
        @pl.when(own_flag[4 + direction])
        def _(direction=direction):
            hand_on(direction, other_piece).start()
    s_copies[1].wait_recv()

    def event(e):
        pair = lax.div(e, 2)
        word = words[0]
        for i in range(1, len(words) - 1):
            word = jnp.where(pair == i, words[i], word)
        code = jnp.where(lax.rem(e, 2) == 0, lax.rem(word, 2048), lax.div(word, 2048))
        piece = lax.rem(code, 64)
        flag = [lax.rem(lax.div(code, 64 << i), 2) == 1 for i in range(5)]
        source = lax.rem(piece, 32)
        return source != chip, piece, source, flag

    row = lax.broadcasted_iota(jnp.int32, (ROWS, HD), 0).astype(f32)
    lanes = lax.broadcasted_iota(jnp.int32, (ROWS, HD), 1)

    def inside(piece):
        bounds = kv[piece, 2 * ROWS : SLOT, :].astype(f32)
        return (row >= bounds[0:1, :]) & (row < bounds[1:2, :])

    for half in range(2):
        qmask[half * ROWS : (half + 1) * ROWS, :] = jnp.where(
            inside(half * 32 + chip) | (lanes >= 4), 0.0, masked_score).astype(bf16)

    def keys_of(piece):
        return jnp.concatenate(
            [kv[piece, 0:ROWS, :], jnp.where(inside(piece), 1.0, 0.0).astype(bf16)], axis=1)

    def scores_of(part, keys):
        rows = slice(part * ROWS, (part + 1) * ROWS)
        queries = jnp.concatenate([qrows[rows, :], qmask[rows, :]], axis=1)
        return lax.dot_general(queries, keys, (((1,), (1,)), ((), ())), preferred_element_type=f32)

    def keep(part, new_max, total, product):
        rows = slice(part * ROWS, (part + 1) * ROWS)
        run_max[rows, :] = jnp.broadcast_to(new_max, (ROWS, HD))
        run_sum[rows, :] = jnp.broadcast_to(total, (ROWS, HD))
        acc[rows, :] = product

    own_keys = [keys_of(chip), keys_of(32 + chip)]
    own_values = [kv[half * 32 + chip, ROWS : 2 * ROWS, :] for half in range(2)]
    q_at = lax.broadcasted_iota(jnp.int32, (ROWS, ROWS), 0)
    k_at = lax.broadcasted_iota(jnp.int32, (ROWS, ROWS), 1)
    for part in range(2):
        scores = [scores_of(part, own_keys[half]) for half in range(part + 1)]
        scores[part] = jnp.where(k_at <= q_at, scores[part], masked_score)
        new_max = jnp.max(scores[part], axis=1, keepdims=True)
        if part == 1:
            new_max = jnp.maximum(new_max, jnp.max(scores[0], axis=1, keepdims=True))
        total, product = 0.0, 0.0
        for half in range(part + 1):
            weights = jnp.exp(scores[half] - new_max)
            total = total + jnp.sum(weights, axis=1, keepdims=True)
            product = product + jnp.dot(
                weights.astype(bf16), own_values[half], preferred_element_type=f32)
        keep(part, new_max, total, product)

    def attend(source):
        keys = jnp.concatenate([keys_of(source), keys_of(32 + source)], axis=0)
        values = jnp.concatenate(
            [kv[half * 32 + source, ROWS : 2 * ROWS, :] for half in range(2)], axis=0)
        queries = jnp.concatenate([qrows[...], qmask[...]], axis=1)
        scores = lax.dot_general(
            queries, keys, (((1,), (1,)), ((), ())), preferred_element_type=f32)
        old_max = run_max[...]
        new_max = jnp.maximum(old_max, jnp.max(scores, axis=1, keepdims=True))
        weights = jnp.exp(scores - jnp.concatenate([new_max] * (BLOCK // HD), axis=1))
        factor = jnp.exp(old_max - new_max)
        run_max[...] = new_max
        run_sum[...] = run_sum[...] * factor + jnp.sum(weights, axis=1, keepdims=True)
        acc[...] = acc[...] * factor + jnp.dot(
            weights.astype(bf16), values, preferred_element_type=f32)

    def step(e, carry):
        valid, piece, source, flag = event(e)

        @pl.when(valid)
        def _():
            hand_on(0, piece).wait_recv()
            for direction in range(4):
                @pl.when(flag[direction])
                def _(direction=direction):
                    hand_on(direction, piece).start()

            @pl.when(flag[4])
            def _():
                attend(source)

        return carry

    lax.fori_loop(0, EVENTS, step, 0)

    for half in range(2):
        rows = slice(half * ROWS, (half + 1) * ROWS)
        ogive[half] = (acc[rows, :] / run_sum[rows, 0:1]).astype(bf16)

    o_copies = []
    lot = head * 2 + core
    for j in (2, 1, 3, 0):
        for c in range(2):
            if j == 0 and c == 0:
                continue
            row_core = core if c == 0 else other
            copy = pltpu.make_async_remote_copy(
                src_ref=ogive.at[row_core], dst_ref=att.at[lot], send_sem=o_send.at[j * 2 + c],
                recv_sem=o_recv.at[lot], device_id=(at(x, z, row_core), y_of[j]), device_id_type=MESH)
            copy.start()
            o_copies.append(copy)
    att[lot] = ogive[core]

    for direction in range(8):
        @pl.when(own_flag[direction])
        def _(direction=direction):
            hand_on(direction % 4, own_piece if direction < 4 else other_piece).wait_send()

    def drain(e, carry):
        valid, piece, source, flag = event(e)
        for direction in range(4):
            @pl.when(flag[direction])
            def _(direction=direction):
                hand_on(direction, piece).wait_send()
        return carry

    lax.fori_loop(0, EVENTS, drain, 0)
    for copy in x_copies + w_copies + s_copies:
        copy.wait_send()

    for j in range(1, 4):
        pltpu.make_async_remote_copy(
            src_ref=wout_hbm.at[:, columns], dst_ref=wcol.at[y_of[j]], send_sem=w_send.at[j],
            recv_sem=w_recv.at[y_of[j]], device_id=(seq, y_of[j]), device_id_type=MESH).wait_recv()
    total = None
    for j in (0, 1, 3, 2):
        for c in range(2):
            if j == 0 and c == 0:
                continue
            lot_of = y_of[j] * 2 + (core if c == 0 else other)
            pltpu.make_async_remote_copy(
                src_ref=ogive.at[core], dst_ref=att.at[lot_of], send_sem=o_send.at[j * 2 + c],
                recv_sem=o_recv.at[lot_of], device_id=partner, device_id_type=MESH).wait_recv()
        both = jnp.concatenate([att[2 * y_of[j]], att[2 * y_of[j] + 1]], axis=1)
        term = jnp.dot(both, wcol[y_of[j]], preferred_element_type=f32)
        total = term if total is None else total + term
    out_ref[...] = total.astype(bf16)

    for copy in o_copies:
        copy.wait_send()


def per_device(face_rows, norm_gain, w_qkv, w_out, segments):
    bf16, f32 = jnp.bfloat16, jnp.float32
    vmem = pl.BlockSpec(memory_space=pltpu.VMEM)
    hbm = pl.BlockSpec(memory_space=pl.ANY)
    dma = pltpu.SemaphoreType.DMA
    return pl.pallas_call(
        kernel,
        name="face_attention",
        out_shape=jax.ShapeDtypeStruct((ROWS, ROWS), bf16),
        in_specs=[hbm, hbm, hbm, hbm, hbm],
        out_specs=vmem,
        scratch_shapes=[
            pltpu.VMEM((4, ROWS, ROWS), bf16),
            pltpu.VMEM((1, 1024), f32),
            pltpu.VMEM((3, 1024, ROWS), bf16),
            pltpu.VMEM((4, ROWS, ROWS), bf16),
            pltpu.VMEM((2, HD), jnp.int32),
            pltpu.VMEM((64, SLOT, HD), bf16),
            pltpu.VMEM((SLOT, HD), bf16),
            pltpu.VMEM((ROWS, HD), bf16),
            pltpu.VMEM((BLOCK, HD), bf16),
            pltpu.VMEM((BLOCK, HD), bf16),
            pltpu.VMEM((BLOCK, HD), f32),
            pltpu.VMEM((BLOCK, HD), f32),
            pltpu.VMEM((BLOCK, HD), f32),
            pltpu.VMEM((2, ROWS, HD), bf16),
            pltpu.VMEM((8, ROWS, HD), bf16),
            dma((5,)),
            dma((4,)), dma((4,)),
            dma((4,)), dma((4,)),
            dma((4,)), dma((4,)),
            dma((4, 64)), dma((64,)),
            dma((8,)), dma((8,)),
        ],
        compiler_params=pltpu.CompilerParams(
            collective_id=0, has_side_effects=True, vmem_limit_bytes=67043328),
    )(
        face_rows,
        norm_gain.reshape(1, 1024),
        jnp.transpose(w_qkv, (1, 0, 2)),
        w_out,
        segments.reshape(2, HD),
    )


def solution(mesh):
    in_specs = (P("seq", "head"), P(), P(None, None, "head"), P("head", None), P("seq"))
    out_specs = P("seq", "head")
    return jax.shard_map(
        per_device, mesh=mesh, in_specs=in_specs, out_specs=out_specs, check_vma=False
    )
```

```python
import functools
import math

import jax
import jax.numpy as jnp
from jax import lax
from jax.experimental import pallas as pl
from jax.experimental.pallas import tpu as pltpu
from jax.sharding import PartitionSpec as P

MESH = pl.DeviceIdType.MESH
HD = 128
epsilon = 1e-05
masked_score = -1e30
PLAN = (
    (788743, 854536, 1585801, 1132930, 600994, 1153101, 564, 0, 0, 0, 0, 0, 0, 0, 0, 0, 0, 0, 0, 247),
    (655490, 1905321, 214368, 1073331, 2573, 2049, 2049, 2049, 2049, 2049, 2049, 2049, 2049, 2049, 2049, 2049, 2049, 2049, 2049, 119),
    (657930, 2820387, 1083456, 2687628, 606387, 4098, 4098, 4098, 4098, 4098, 4098, 4098, 4098, 4098, 4098, 4098, 4098, 4098, 4098, 123),
    (659748, 1138018, 1335827, 657964, 1086561, 1141056, 7264, 6147, 6147, 6147, 6147, 6147, 6147, 6147, 6147, 6147, 6147, 6147, 6147, 181),
    (286787, 1156451, 528941, 2298451, 2820353, 1079552, 9248, 8196, 8196, 8196, 8196, 8196, 8196, 8196, 8196, 8196, 8196, 8196, 8196, 125),
    (139789, 2826797, 2824515, 594575, 595, 593184, 1084417, 11266, 10245, 10245, 10245, 10245, 10245, 10245, 10245, 10245, 10245, 10245, 10245, 217),
    (665863, 2828847, 1341517, 663936, 2303136, 788547, 1082401, 543284, 1148195, 1087490, 13346, 12294, 12294, 12294, 12294, 12294, 12294, 12294, 12294, 213),
    (786758, 2425391, 265254, 2427141, 266377, 158821, 533922, 531748, 15395, 14343, 14343, 14343, 14343, 14343, 14343, 14343, 14343, 14343, 14343, 203),
    (346761, 2424832, 806983, 2951553, 2308166, 530562, 2432358, 142370, 1155332, 2696549, 16392, 16392, 16392, 16392, 16392, 16392, 16392, 16392, 16392, 127),
    (147850, 3624, 525601, 268322, 2162759, 669091, 2833410, 368772, 2700708, 2697221, 18441, 18441, 18441, 18441, 18441, 18441, 18441, 18441, 18441, 247),
    (69705, 1084777, 2435, 2431048, 2296834, 2957444, 669792, 144424, 2098471, 77094, 21509, 20490, 20490, 20490, 20490, 20490, 20490, 20490, 20490, 91),
    (1087939, 1138762, 1086826, 4228, 1665353, 2170276, 2168169, 540673, 11297, 340096, 3343525, 2179143, 2110759, 22539, 22539, 22539, 22539, 22539, 22539, 213),
    (551243, 1155268, 2695853, 1088619, 2168835, 135498, 272390, 2962538, 2435145, 16385, 343145, 1057, 2167840, 2112552, 24588, 24588, 24588, 24588, 24588, 125),
    (76140, 154700, 205190, 2108582, 279556, 867691, 151619, 2183746, 1250, 1084840, 19491, 2182176, 3079, 27681, 26637, 26637, 26637, 26637, 26637, 251),
    (1145222, 1731343, 2569325, 803143, 10572, 2964588, 2305448, 1155600, 678016, 8752, 2162985, 265252, 2316291, 2165795, 4106, 2167817, 29738, 28686, 28686, 68),
    (473480, 13480, 18701, 2713600, 2307241, 2111502, 666784, 545036, 3372, 2173998, 5281, 2166795, 8739, 2186410, 2104356, 30735, 30735, 30735, 30735, 230),
    (147857, 3097009, 686112, 281711, 146601, 2177290, 2969665, 12622, 2166126, 284674, 6413, 142701, 2098214, 2448418, 8204, 2173987, 2171948, 32784, 32784, 119),
    (164233, 2444656, 147731, 2969866, 1315944, 2297889, 686219, 1679488, 2448751, 2562051, 8199, 2177094, 91137, 2121742, 2716710, 93220, 2123781, 35877, 34833, 119),
    (1214867, 1315242, 810353, 893008, 85163, 2118768, 268296, 2310276, 2166956, 2171397, 2121807, 146441, 2324494, 2169133, 2911271, 2172934, 2192422, 36882, 36882, 85),
    (809554, 2855348, 1121515, 165900, 271363, 2852970, 689324, 272585, 354446, 2172208, 2436237, 1262697, 2978888, 31754, 12295, 2176047, 39975, 38931, 38931, 91),
    (942675, 2856964, 155052, 1321298, 2855054, 2185357, 2172581, 2978129, 2314442, 2189446, 2438513, 620560, 2195465, 2313231, 81959, 2245639, 40980, 40980, 40980, 181),
    (92500, 1059214, 2436468, 2977875, 2121836, 2123814, 558214, 23923, 561167, 2317743, 1215858, 343216, 22151, 2722922, 81929, 2114601, 43029, 43029, 43029, 85),
    (698830, 2338286, 2109478, 696976, 2455695, 28276, 278192, 90195, 16689, 2123123, 88201, 2190375, 2179122, 21521, 2182155, 2184210, 45078, 45078, 45078, 85),
    (686480, 570607, 2732103, 2309552, 16974, 3371025, 568497, 2179149, 281653, 42221, 2203717, 156713, 563754, 2727050, 2318482, 2199563, 48171, 47127, 47127, 68),
    (313424, 379424, 17456, 297047, 2340873, 300209, 2179590, 2127919, 2182322, 2338902, 1118218, 159763, 2192426, 88085, 2205805, 2123788, 2120755, 2187284, 50228, 51),
    (180241, 2198648, 18578, 2181200, 2327074, 179378, 2341011, 21555, 1335467, 162858, 2325643, 176180, 2339860, 2449429, 27701, 2189326, 52270, 51225, 51225, 51),
    (299522, 2345049, 1070258, 180243, 2184627, 2342961, 32939, 1074315, 2195604, 306257, 2203735, 2342060, 46261, 2127919, 95286, 2123821, 54286, 53274, 53274, 17),
    (1120346, 2347187, 23044, 183467, 2203796, 306195, 25721, 2449458, 2467928, 2134065, 2189325, 164920, 2131990, 48240, 291894, 2210990, 2193423, 55323, 55323, 17),
    (303748, 1058907, 306299, 24666, 105653, 2204794, 2187405, 3237913, 37014, 291961, 50226, 2469905, 47759, 33838, 2212913, 2327571, 2210991, 57372, 57372, 17),
    (305797, 1124444, 2352373, 41510, 187021, 2189462, 2349198, 2470964, 2191450, 2347159, 32783, 104472, 168979, 117944, 2200623, 2149559, 2195505, 60433, 59421, 17),
    (307878, 2353245, 2469980, 28823, 43160, 2475125, 2351151, 173071, 2473006, 313435, 101499, 2213978, 104464, 2335761, 2348080, 2134066, 62483, 61470, 61470, 17),
    (440839, 311847, 2603038, 2475070, 313360, 59407, 2223215, 2476118, 58486, 298032, 175153, 1086581, 2221746, 172051, 56371, 54331, 2204730, 63519, 63519, 0),
    (1130657, 1077775, 858241, 266761, 332334, 1073707, 610860, 66093, 65568, 65568, 65568, 65568, 65568, 65568, 65568, 65568, 65568, 65568, 65568, 119),
    (197161, 2752898, 1083555, 1399338, 1142946, 1401392, 68492, 67617, 67617, 67617, 67617, 67617, 67617, 67617, 67617, 67617, 67617, 67617, 67617, 119),
    (1397155, 1398881, 1072449, 1138720, 288064, 69666, 69666, 69666, 69666, 69666, 69666, 69666, 69666, 69666, 69666, 69666, 69666, 69666, 69666, 181),
    (1137444, 1401186, 200002, 1140876, 537921, 1077312, 1084448, 72207, 71715, 71715, 71715, 71715, 71715, 71715, 71715, 71715, 71715, 71715, 71715, 91),
    (727333, 1140035, 274572, 201261, 1339957, 328770, 2164737, 1084303, 74752, 73764, 73764, 73764, 73764, 73764, 73764, 73764, 73764, 73764, 73764, 151),
    (1403270, 1419620, 204100, 1339552, 1342787, 2621538, 2232577, 77089, 75813, 75813, 75813, 75813, 75813, 75813, 75813, 75813, 75813, 75813, 75813, 87),
    (731694, 1145486, 243525, 852589, 1341540, 2884676, 596501, 2759073, 2361634, 78850, 77862, 77862, 77862, 77862, 77862, 77862, 77862, 77862, 77862, 53),
    (78511, 1472672, 2635136, 1208872, 600225, 2632240, 1081910, 2361869, 529261, 71716, 2167346, 2104580, 80404, 79911, 79911, 79911, 79911, 79911, 79911, 68),
    (555488, 1274505, 736512, 2242594, 602497, 2625835, 335174, 75812, 2366625, 349445, 82948, 81960, 81960, 81960, 81960, 81960, 81960, 81960, 81960, 127),
    (1083496, 1904993, 2245761, 1147051, 196899, 1663854, 212098, 336896, 2890823, 12325, 2107660, 2700676, 84009, 84009, 84009, 84009, 84009, 84009, 84009, 125),
    (1399202, 1595753, 2771107, 860588, 2365537, 2102273, 196936, 862509, 211246, 2893127, 2229381, 537704, 87462, 86058, 86058, 86058, 86058, 86058, 86058, 93),
    (217772, 336259, 201802, 740269, 2232485, 2169929, 200069, 2231428, 2371750, 1083656, 604192, 2098439, 89128, 88107, 88107, 88107, 88107, 88107, 88107, 127),
    (743597, 2251044, 553125, 2894051, 2103402, 2367750, 2962506, 79970, 606313, 2636866, 556105, 68113, 2100488, 2162688, 90156, 90156, 90156, 90156, 90156, 207),
    (600629, 745774, 2369678, 2437510, 743524, 2251175, 345156, 2252835, 2898947, 2900330, 263498, 70816, 67881, 2100226, 93193, 92205, 92205, 92205, 92205, 95),
    (1141222, 867661, 10664, 2898453, 328840, 678252, 2316388, 2098252, 18530, 2173954, 86017, 2106401, 7178, 2182150, 95267, 94254, 94254, 94254, 94254, 251),
    (997742, 3175080, 2901447, 209456, 1081376, 1076224, 806086, 264293, 1152069, 615465, 267309, 22563, 2165028, 2105876, 2186243, 2121738, 2184226, 96303, 96303, 156),
    (886888, 365896, 2127983, 169, 824352, 210990, 2243105, 2230666, 88098, 2116622, 77859, 2102442, 2381868, 2241548, 93187, 11277, 9253, 99364, 98352, 119),
    (346546, 1278098, 2261034, 2905353, 331937, 2113640, 465922, 94575, 210987, 2119852, 2128903, 2365476, 617473, 2122766, 2367653, 78853, 2124806, 100401, 100401, 151),
    (624874, 2788554, 3412002, 84011, 2120048, 7504, 549961, 214060, 2113700, 27683, 97709, 2369765, 618535, 2106375, 13326, 2128934, 102450, 102450, 102450, 119),
    (350578, 2658339, 91211, 2365482, 2908196, 93258, 1215492, 216205, 272688, 619792, 83057, 2247688, 79878, 2389029, 2112550, 2127919, 104499, 104499, 104499, 85),
    (352627, 3039277, 1320275, 627853, 75819, 881700, 2126923, 622602, 275461, 80465, 2135206, 84143, 2129960, 2329615, 2114602, 2112521, 106548, 106548, 106548, 85),
    (762029, 2794893, 356517, 2125939, 884780, 144972, 2792486, 342123, 2119855, 2112656, 2108431, 166058, 2179144, 37898, 2199593, 2116657, 108597, 108597, 108597, 89),
    (764046, 886357, 2191526, 2916527, 80244, 2793485, 155781, 1133583, 823464, 2986323, 220297, 2333703, 2110508, 87048, 101387, 2118673, 111661, 110646, 110646, 85),
    (1409135, 3440694, 226582, 362535, 2242613, 2128562, 2664456, 2126505, 2921673, 631848, 1332756, 155661, 2321452, 205994, 2132243, 2119723, 113715, 112695, 112695, 68),
    (313529, 2261040, 81961, 362615, 102447, 105559, 1209423, 2134170, 2395144, 2115670, 2192170, 108587, 3169290, 2136653, 106540, 2272310, 2122772, 115757, 114744, 51),
    (245809, 346266, 365656, 32947, 2135185, 349193, 244267, 2249875, 3431472, 2275374, 90292, 2325007, 3175572, 177164, 93238, 110093, 117781, 116793, 116793, 51),
    (102521, 367106, 2397273, 245802, 2398321, 2512939, 2278417, 90292, 2400304, 44048, 2121847, 2117814, 93271, 228365, 2143413, 2191374, 120335, 118842, 118842, 49),
    (367139, 2398330, 2282020, 102443, 247988, 2400300, 2280530, 2121877, 92216, 1280182, 2386955, 99416, 2467895, 2130574, 2133014, 1342510, 2194519, 120891, 120891, 17),
    (368763, 2400772, 236635, 305274, 2187276, 2281654, 93203, 2386041, 2467954, 2405906, 2191374, 113753, 231439, 49200, 2212911, 2145297, 123920, 122940, 122940, 17),
    (305276, 373852, 92212, 2386043, 2206870, 2139227, 2125870, 98419, 1079479, 2136186, 2456666, 376889, 2148402, 101399, 2393112, 2133010, 124989, 124989, 124989, 17),
    (897149, 2288790, 375470, 254990, 240303, 1059000, 99420, 1141911, 2408571, 3177616, 107611, 2138169, 236565, 250905, 2150449, 2394258, 2200595, 127038, 127038, 17),
    (127223, 2537656, 2408559, 3177502, 378941, 2410582, 98830, 240168, 2272272, 363085, 2156572, 2338875, 107053, 53298, 2154129, 2220051, 2139154, 2202682, 129087, 0),
)
EVENTS = 2 * (len(PLAN[0]) - 1)
ROWS = 256
BLOCK = 512
INFO = 16
SLOT = 2 * ROWS + INFO


def pick(values, index):
    result = jnp.int32(values[0])
    for at in range(1, len(values)):
        result = jnp.where(index == at, jnp.int32(values[at]), result)
    return result


def kernel(
    x_hbm, gain_hbm, wqkv_hbm, wout_hbm, seg_hbm, out_ref,
    xbuf, gain_ref, wqkv, wcol, seg_ref, kv, give, qgive, qrows, qmask, acc, run_max, run_sum, ogive, att,
    local_sem, x_send, x_recv, w_send, w_recv, s_send, s_recv, kv_send, kv_recv, o_send, o_recv,
):
    f32, bf16 = jnp.float32, jnp.bfloat16
    seq, head = lax.axis_index("seq"), lax.axis_index("head")
    core = lax.rem(seq, 2)
    chip = lax.div(seq, 2)
    z = lax.rem(chip, 8)
    x = lax.div(chip, 8)
    other = 1 - core

    def at(xx, zz, cc):
        return (xx * 8 + zz) * 2 + cc

    z_up, z_down = lax.rem(z + 1, 8), lax.rem(z + 7, 8)
    x_up, x_down = lax.rem(x + 1, 4), lax.rem(x + 3, 4)
    up = (at(x, z_up, core), head)
    down = (at(x, z_down, core), head)
    right = (at(x_up, z, core), head)
    left = (at(x_down, z, core), head)
    partner = (at(x, z, other), head)
    y_of = [lax.rem(head + j, 4) for j in range(4)]

    barrier = pltpu.get_barrier_semaphore()
    greeted = [up, down, right, left, partner]
    for j in range(1, 4):
        greeted.append((seq, y_of[j]))
        greeted.append((at(x, z, other), y_of[j]))
    for device in greeted:
        pl.semaphore_signal(barrier, inc=1, device_id=device, device_id_type=MESH)

    seg_in = pltpu.make_async_copy(seg_hbm, seg_ref, local_sem.at[3])
    seg_in.start()
    gain_in = pltpu.make_async_copy(gain_hbm, gain_ref, local_sem.at[4])
    gain_in.start()
    mine = pltpu.make_async_copy(x_hbm, xbuf.at[head], local_sem.at[0])
    mine.start()
    weights_in = pltpu.make_async_copy(wqkv_hbm, wqkv, local_sem.at[1])
    weights_in.start()
    columns = pl.ds(pl.multiple_of(head * ROWS, ROWS), ROWS)
    wcol_in = pltpu.make_async_copy(wout_hbm.at[:, columns], wcol.at[head], local_sem.at[2])
    wcol_in.start()

    pl.semaphore_wait(barrier, len(greeted))

    x_copies = []
    for j in (2, 1, 3):
        copy = pltpu.make_async_remote_copy(
            src_ref=x_hbm, dst_ref=xbuf.at[head], send_sem=x_send.at[j], recv_sem=x_recv.at[head],
            device_id=(seq, y_of[j]), device_id_type=MESH)
        copy.start()
        x_copies.append(copy)
    seg_in.wait()
    seg = seg_ref[...]
    lane = lax.broadcasted_iota(jnp.int32, (1, HD), 1)
    sub = lax.broadcasted_iota(jnp.int32, (INFO, HD), 0)
    lower = jnp.zeros((1, HD), f32)
    upper = jnp.zeros((1, HD), f32)
    for t in range(1, 5):
        before = jnp.sum(jnp.where(seg < t, 1.0, 0.0).astype(f32), axis=1, keepdims=True)
        before = before[0:1] + before[1:2]
        lower = jnp.where(lane == t, before, lower)
        upper = jnp.where(lane == t - 1, before, upper)
    lower = jnp.where(lane < 4, lower, 0.0)
    info = jnp.where(sub == 0, lower, jnp.where(sub == 1, upper, 0.0)).astype(bf16)

    mine_at = core * 32 + chip
    words = [pick([row[i] for row in PLAN], mine_at) for i in range(len(PLAN[0]))]
    gain_in.wait()
    mine.wait()
    weights_in.wait()
    wcol_in.wait()
    for j in range(1, 4):
        pltpu.make_async_remote_copy(
            src_ref=x_hbm, dst_ref=xbuf.at[y_of[j]], send_sem=x_send.at[j], recv_sem=x_recv.at[y_of[j]],
            device_id=(seq, y_of[j]), device_id_type=MESH).wait_recv()

    w_copies = []
    for j in range(1, 4):
        theirs = pl.ds(pl.multiple_of(y_of[j] * ROWS, ROWS), ROWS)
        copy = pltpu.make_async_remote_copy(
            src_ref=wout_hbm.at[:, theirs], dst_ref=wcol.at[head], send_sem=w_send.at[j],
            recv_sem=w_recv.at[head], device_id=(seq, y_of[j]), device_id_type=MESH)
        copy.start()
        w_copies.append(copy)

    parts = [xbuf[y].astype(f32) for y in range(4)]
    squares = sum(jnp.sum(part * part, axis=1, keepdims=True) for part in parts)
    scale = lax.rsqrt(squares * (1.0 / 1024.0) + epsilon)
    normed = jnp.concatenate(
        [(parts[y] * scale * gain_ref[:, y * ROWS : (y + 1) * ROWS]).astype(bf16) for y in range(4)], axis=1)

    def project(which):
        return jnp.dot(normed, wqkv[which], preferred_element_type=f32)

    def hand_on(direction, piece):
        device = (up, down, right, left)[direction]
        return pltpu.make_async_remote_copy(
            src_ref=kv.at[piece], dst_ref=kv.at[piece], send_sem=kv_send.at[direction, piece],
            recv_sem=kv_recv.at[piece], device_id=device, device_id_type=MESH)

    own = pl.ds(pl.multiple_of(core * ROWS, ROWS), ROWS)
    own_piece = core * 32 + chip
    other_piece = other * 32 + chip

    def swap(j, source, target, landing):
        return pltpu.make_async_remote_copy(
            src_ref=source, dst_ref=target, send_sem=s_send.at[j], recv_sem=landing,
            device_id=partner, device_id_type=MESH)

    give[2 * ROWS : SLOT, :] = info
    kv[own_piece, 2 * ROWS : SLOT, :] = info
    for j in (1, 2):
        both = project(j).astype(bf16)
        first, second = both[:, :HD], both[:, HD:]
        give[(j - 1) * ROWS : j * ROWS, :] = jnp.where(core == 0, second, first)
        kv[own_piece, (j - 1) * ROWS : j * ROWS, :] = jnp.where(core == 0, first, second)

    own_flag = [lax.rem(lax.div(words[-1], 1 << i), 2) == 1 for i in range(8)]
    s_copies = [swap(0, give, kv.at[own_piece], kv_recv.at[own_piece])]
    s_copies[0].start()
    for direction in range(4):
        @pl.when(own_flag[direction])
        def _(direction=direction):
            hand_on(direction, own_piece).start()

    both = (project(0) * (1.0 / math.sqrt(HD))).astype(bf16)
    first, second = both[:, :HD], both[:, HD:]
    qgive[...] = jnp.where(core == 0, second, first)
    s_copies.append(swap(1, qgive, qrows.at[own], s_recv.at[1]))
    s_copies[1].start()
    qrows[own, :] = jnp.where(core == 0, first, second)

    swap(0, give, kv.at[other_piece], kv_recv.at[other_piece]).wait_recv()
    for direction in range(4):
        @pl.when(own_flag[4 + direction])
        def _(direction=direction):
            hand_on(direction, other_piece).start()
    s_copies[1].wait_recv()

    def event(e):
        pair = lax.div(e, 2)
        word = words[0]
        for i in range(1, len(words) - 1):
            word = jnp.where(pair == i, words[i], word)
        code = jnp.where(lax.rem(e, 2) == 0, lax.rem(word, 2048), lax.div(word, 2048))
        piece = lax.rem(code, 64)
        flag = [lax.rem(lax.div(code, 64 << i), 2) == 1 for i in range(5)]
        source = lax.rem(piece, 32)
        return source != chip, piece, source, flag

    row = lax.broadcasted_iota(jnp.int32, (ROWS, HD), 0).astype(f32)
    lanes = lax.broadcasted_iota(jnp.int32, (ROWS, HD), 1)

    def inside(piece):
        bounds = kv[piece, 2 * ROWS : SLOT, :].astype(f32)
        return (row >= bounds[0:1, :]) & (row < bounds[1:2, :])

    for half in range(2):
        qmask[half * ROWS : (half + 1) * ROWS, :] = jnp.where(
            inside(half * 32 + chip) | (lanes >= 4), 0.0, masked_score).astype(bf16)

    def keys_of(piece):
        return jnp.concatenate(
            [kv[piece, 0:ROWS, :], jnp.where(inside(piece), 1.0, 0.0).astype(bf16)], axis=1)

    def scores_of(part, keys):
        rows = slice(part * ROWS, (part + 1) * ROWS)
        queries = jnp.concatenate([qrows[rows, :], qmask[rows, :]], axis=1)
        return lax.dot_general(queries, keys, (((1,), (1,)), ((), ())), preferred_element_type=f32)

    def keep(part, new_max, total, product):
        rows = slice(part * ROWS, (part + 1) * ROWS)
        run_max[rows, :] = jnp.broadcast_to(new_max, (ROWS, HD))
        run_sum[rows, :] = jnp.broadcast_to(total, (ROWS, HD))
        acc[rows, :] = product

    own_keys = [keys_of(chip), keys_of(32 + chip)]
    own_values = [kv[half * 32 + chip, ROWS : 2 * ROWS, :] for half in range(2)]
    q_at = lax.broadcasted_iota(jnp.int32, (ROWS, ROWS), 0)
    k_at = lax.broadcasted_iota(jnp.int32, (ROWS, ROWS), 1)
    for part in range(2):
        scores = [scores_of(part, own_keys[half]) for half in range(part + 1)]
        scores[part] = jnp.where(k_at <= q_at, scores[part], masked_score)
        new_max = jnp.max(scores[part], axis=1, keepdims=True)
        if part == 1:
            new_max = jnp.maximum(new_max, jnp.max(scores[0], axis=1, keepdims=True))
        total, product = 0.0, 0.0
        for half in range(part + 1):
            weights = jnp.exp(scores[half] - new_max)
            total = total + jnp.sum(weights, axis=1, keepdims=True)
            product = product + jnp.dot(
                weights.astype(bf16), own_values[half], preferred_element_type=f32)
        keep(part, new_max, total, product)

    def attend(source):
        keys = jnp.concatenate([keys_of(source), keys_of(32 + source)], axis=0)
        values = jnp.concatenate(
            [kv[half * 32 + source, ROWS : 2 * ROWS, :] for half in range(2)], axis=0)
        queries = jnp.concatenate([qrows[...], qmask[...]], axis=1)
        scores = lax.dot_general(
            queries, keys, (((1,), (1,)), ((), ())), preferred_element_type=f32)
        old_max = run_max[...]
        new_max = jnp.maximum(old_max, jnp.max(scores, axis=1, keepdims=True))
        weights = jnp.exp(scores - jnp.concatenate([new_max] * (BLOCK // HD), axis=1))
        factor = jnp.exp(old_max - new_max)
        run_max[...] = new_max
        run_sum[...] = run_sum[...] * factor + jnp.sum(weights, axis=1, keepdims=True)
        acc[...] = acc[...] * factor + jnp.dot(
            weights.astype(bf16), values, preferred_element_type=f32)

    def step(e, carry):
        valid, piece, source, flag = event(e)

        @pl.when(valid)
        def _():
            hand_on(0, piece).wait_recv()
            for direction in range(4):
                @pl.when(flag[direction])
                def _(direction=direction):
                    hand_on(direction, piece).start()

            @pl.when(flag[4])
            def _():
                attend(source)

        return carry

    lax.fori_loop(0, EVENTS, step, 0)

    for half in range(2):
        rows = slice(half * ROWS, (half + 1) * ROWS)
        ogive[half] = (acc[rows, :] / run_sum[rows, 0:1]).astype(bf16)

    o_copies = []
    lot = head * 2 + core
    for j in (2, 1, 3, 0):
        for c in range(2):
            if j == 0 and c == 0:
                continue
            row_core = core if c == 0 else other
            copy = pltpu.make_async_remote_copy(
                src_ref=ogive.at[row_core], dst_ref=att.at[lot], send_sem=o_send.at[j * 2 + c],
                recv_sem=o_recv.at[lot], device_id=(at(x, z, row_core), y_of[j]), device_id_type=MESH)
            copy.start()
            o_copies.append(copy)
    att[lot] = ogive[core]

    for direction in range(8):
        @pl.when(own_flag[direction])
        def _(direction=direction):
            hand_on(direction % 4, own_piece if direction < 4 else other_piece).wait_send()

    def drain(e, carry):
        valid, piece, source, flag = event(e)
        for direction in range(4):
            @pl.when(flag[direction])
            def _(direction=direction):
                hand_on(direction, piece).wait_send()
        return carry

    lax.fori_loop(0, EVENTS, drain, 0)
    for copy in x_copies + w_copies + s_copies:
        copy.wait_send()

    for j in range(1, 4):
        pltpu.make_async_remote_copy(
            src_ref=wout_hbm.at[:, columns], dst_ref=wcol.at[y_of[j]], send_sem=w_send.at[j],
            recv_sem=w_recv.at[y_of[j]], device_id=(seq, y_of[j]), device_id_type=MESH).wait_recv()
    total = None
    for j in (0, 1, 3, 2):
        for c in range(2):
            if j == 0 and c == 0:
                continue
            lot_of = y_of[j] * 2 + (core if c == 0 else other)
            pltpu.make_async_remote_copy(
                src_ref=ogive.at[core], dst_ref=att.at[lot_of], send_sem=o_send.at[j * 2 + c],
                recv_sem=o_recv.at[lot_of], device_id=partner, device_id_type=MESH).wait_recv()
        both = jnp.concatenate([att[2 * y_of[j]], att[2 * y_of[j] + 1]], axis=1)
        term = jnp.dot(both, wcol[y_of[j]], preferred_element_type=f32)
        total = term if total is None else total + term
    out_ref[...] = total.astype(bf16)

    for copy in o_copies:
        copy.wait_send()


def per_device(face_rows, norm_gain, w_qkv, w_out, segments):
    bf16, f32 = jnp.bfloat16, jnp.float32
    vmem = pl.BlockSpec(memory_space=pltpu.VMEM)
    hbm = pl.BlockSpec(memory_space=pl.ANY)
    dma = pltpu.SemaphoreType.DMA
    return pl.pallas_call(
        kernel,
        name="face_attention",
        out_shape=jax.ShapeDtypeStruct((ROWS, ROWS), bf16),
        in_specs=[hbm, hbm, hbm, hbm, hbm],
        out_specs=vmem,
        scratch_shapes=[
            pltpu.VMEM((4, ROWS, ROWS), bf16),
            pltpu.VMEM((1, 1024), f32),
            pltpu.VMEM((3, 1024, ROWS), bf16),
            pltpu.VMEM((4, ROWS, ROWS), bf16),
            pltpu.VMEM((2, HD), jnp.int32),
            pltpu.VMEM((64, SLOT, HD), bf16),
            pltpu.VMEM((SLOT, HD), bf16),
            pltpu.VMEM((ROWS, HD), bf16),
            pltpu.VMEM((BLOCK, HD), bf16),
            pltpu.VMEM((BLOCK, HD), bf16),
            pltpu.VMEM((BLOCK, HD), f32),
            pltpu.VMEM((BLOCK, HD), f32),
            pltpu.VMEM((BLOCK, HD), f32),
            pltpu.VMEM((2, ROWS, HD), bf16),
            pltpu.VMEM((8, ROWS, HD), bf16),
            dma((5,)),
            dma((4,)), dma((4,)),
            dma((4,)), dma((4,)),
            dma((4,)), dma((4,)),
            dma((4, 64)), dma((64,)),
            dma((8,)), dma((8,)),
        ],
        compiler_params=pltpu.CompilerParams(
            collective_id=0, has_side_effects=True, vmem_limit_bytes=67043328),
    )(
        face_rows,
        norm_gain.reshape(1, 1024),
        jnp.transpose(w_qkv, (1, 0, 2)),
        w_out,
        segments.reshape(2, HD),
    )


def solution(mesh):
    in_specs = (P("seq", "head"), P(), P(None, None, "head"), P("head", None), P("seq"))
    out_specs = P("seq", "head")
    return jax.shard_map(
        per_device, mesh=mesh, in_specs=in_specs, out_specs=out_specs, check_vma=False
    )
```

```python
import functools
import math

import jax
import jax.numpy as jnp
from jax import lax
from jax.experimental import pallas as pl
from jax.experimental.pallas import tpu as pltpu
from jax.sharding import PartitionSpec as P

MESH = pl.DeviceIdType.MESH
HD = 128
epsilon = 1e-05
masked_score = -1e30
PLAN = (
    (1065223, 854657, 1061385, 332162, 1069317, 1141292, 524, 0, 0, 0, 0, 0, 0, 0, 0, 0, 0, 0, 0, 247),
    (131593, 1133442, 1069474, 1137760, 1335980, 2049, 2049, 2049, 2049, 2049, 2049, 2049, 2049, 2049, 2049, 2049, 2049, 2049, 2049, 119),
    (133642, 598307, 656481, 1402208, 1140876, 4660, 4098, 4098, 4098, 4098, 4098, 4098, 4098, 4098, 4098, 4098, 4098, 4098, 4098, 123),
    (1071170, 1137060, 2822796, 658092, 2820653, 2294016, 6705, 6147, 6147, 6147, 6147, 6147, 6147, 6147, 6147, 6147, 6147, 6147, 6147, 117),
    (662156, 2824876, 660141, 2822950, 1157377, 590945, 9216, 8196, 8196, 8196, 8196, 8196, 8196, 8196, 8196, 8196, 8196, 8196, 8196, 125),
    (1075524, 2826662, 1587523, 525411, 1144834, 2163746, 2099233, 10245, 10245, 10245, 10245, 10245, 10245, 10245, 10245, 10245, 10245, 10245, 10245, 85),
    (665991, 1143310, 787557, 139791, 2949807, 138596, 2689025, 2824450, 13602, 12294, 12294, 12294, 12294, 12294, 12294, 12294, 12294, 12294, 12294, 181),
    (786502, 2699791, 667040, 2427009, 1082661, 8578, 2696610, 223235, 15395, 14343, 14343, 14343, 14343, 14343, 14343, 14343, 14343, 14343, 14343, 75),
    (131721, 2294666, 264295, 2952263, 2830406, 268613, 2166786, 2829475, 2171140, 16392, 16392, 16392, 16392, 16392, 16392, 16392, 16392, 16392, 16392, 127),
    (789130, 2310216, 2820907, 792642, 2955623, 2428960, 668672, 2242724, 2831492, 616517, 19493, 18441, 18441, 18441, 18441, 18441, 18441, 18441, 18441, 223),
    (673963, 595305, 2955651, 67912, 861288, 1403444, 1412, 2101607, 2100256, 600326, 2176071, 21765, 20490, 20490, 20490, 20490, 20490, 20490, 20490, 91),
    (151939, 615715, 599402, 354633, 2367522, 265321, 1149256, 2835553, 337920, 2699526, 2111783, 2163714, 23557, 22539, 22539, 22539, 22539, 22539, 22539, 189),
    (270411, 2171821, 863595, 6709, 2300234, 274697, 2438506, 2494562, 133423, 2296937, 1048583, 2703624, 2370720, 25895, 24588, 24588, 24588, 24588, 24588, 185),
    (680197, 2842805, 603621, 2371652, 2170955, 2841007, 137351, 540800, 2439242, 2704419, 2838530, 1050633, 2163746, 2165801, 26637, 26637, 26637, 26637, 26637, 125),
    (158150, 1407759, 15725, 680328, 2439173, 2176364, 2965504, 140325, 2425225, 2123, 2841636, 7201, 544770, 2184227, 2182178, 28686, 28686, 28686, 28686, 204),
    (997768, 1082792, 524358, 2111625, 552038, 28938, 3763232, 10369, 549989, 2165806, 5164, 6148, 2171939, 2166795, 2186409, 31786, 30735, 30735, 30735, 110),
    (297032, 2834609, 65615, 281967, 2119, 153001, 2177358, 2166126, 5546, 875520, 2906150, 551942, 2304069, 7213, 2167843, 2170884, 2187276, 32784, 32784, 119),
    (280656, 2852009, 266666, 630888, 350543, 146799, 2099233, 2114699, 2117763, 29735, 91299, 2323618, 336141, 2105446, 2122797, 76806, 35845, 34833, 34833, 119),
    (690451, 2328746, 688820, 2851211, 6146, 352361, 2429987, 288808, 336207, 2325636, 2115655, 2117902, 2186279, 2192429, 2114572, 12325, 2108454, 36882, 36882, 85),
    (692427, 2330804, 559107, 9251, 353905, 86157, 164907, 2122852, 816432, 2312201, 2451464, 2180106, 12325, 556078, 2108454, 80943, 39943, 38931, 38931, 87),
    (270675, 814451, 88402, 24718, 2251890, 414764, 2977957, 3418417, 558125, 149510, 2184209, 2182192, 30727, 82991, 2171912, 2176039, 40980, 40980, 40980, 117),
    (289108, 2714996, 272526, 2977875, 25971, 2187398, 2173200, 2174994, 2330767, 2194608, 88263, 2250769, 2177032, 2179082, 19505, 2184233, 43029, 43029, 43029, 212),
    (764110, 275694, 820774, 96340, 2983055, 93556, 822293, 16723, 2857127, 2983948, 2180204, 102569, 2116615, 23565, 87083, 2135050, 45078, 45078, 45078, 69),
    (569423, 3111568, 2982471, 16974, 108945, 2460903, 566894, 2208808, 2727945, 38976, 421545, 2140170, 2321459, 3493906, 88140, 2319410, 48139, 47127, 47127, 68),
    (163993, 2196000, 16569, 1050711, 2179089, 2340873, 300209, 176646, 97458, 21519, 2181267, 160886, 2323635, 2183189, 88108, 224373, 41995, 2124812, 50228, 51),
    (297048, 2591234, 2343058, 99506, 18579, 179241, 2131063, 218291, 176171, 2117743, 2119828, 2128950, 2466316, 43118, 2187277, 2206734, 52269, 51225, 51225, 51),
    (1052818, 2592857, 302201, 2464266, 180241, 2197652, 1137784, 90192, 3170391, 306315, 2196599, 93226, 2203663, 46093, 29750, 2206767, 54318, 53274, 53274, 17),
    (39002, 2348211, 303193, 36875, 2331700, 167595, 1336441, 49301, 1141804, 2342934, 2471053, 2197520, 48240, 2467854, 2192439, 2127919, 55323, 55323, 55323, 17),
    (303620, 2465883, 2349580, 306732, 184403, 2348083, 182317, 1126550, 2471053, 2134130, 49745, 2346165, 2453518, 2211863, 359537, 33807, 2210928, 57372, 57372, 17),
    (188629, 2206844, 26774, 172123, 2204854, 1064059, 291885, 2191379, 184472, 359475, 2347159, 2390032, 2471961, 2211890, 2213905, 2135089, 60464, 59421, 59421, 17),
    (307293, 2601510, 291965, 1222808, 2192501, 188567, 292880, 2473007, 2196604, 107704, 35860, 186393, 2201619, 2350137, 1348657, 2347098, 62514, 61470, 61470, 17),
    (311815, 61655, 2604216, 314430, 59478, 2193487, 2477686, 2222128, 2197521, 41557, 1348624, 2204789, 59058, 55315, 2202684, 54331, 64570, 63519, 63519, 0),
    (1065377, 1585679, 487586, 1077667, 1137162, 1134892, 1075492, 65568, 65568, 65568, 65568, 65568, 65568, 65568, 65568, 65568, 65568, 65568, 65568, 119),
    (331872, 859456, 1401514, 1073710, 67617, 67617, 67617, 67617, 67617, 67617, 67617, 67617, 67617, 67617, 67617, 67617, 67617, 67617, 67617, 87),
    (723875, 1151658, 1133889, 1401184, 2228755, 69772, 69666, 69666, 69666, 69666, 69666, 69666, 69666, 69666, 69666, 69666, 69666, 69666, 69666, 151),
    (1136994, 1088834, 199308, 1142081, 1089568, 73024, 71715, 71715, 71715, 71715, 71715, 71715, 71715, 71715, 71715, 71715, 71715, 71715, 71715, 91),
    (2824515, 201261, 1143444, 593218, 2099488, 1147904, 73764, 73764, 73764, 73764, 73764, 73764, 73764, 73764, 73764, 73764, 73764, 73764, 73764, 213),
    (1403174, 2236772, 1061389, 1405492, 2824259, 725152, 2757632, 1146913, 77057, 75813, 75813, 75813, 75813, 75813, 75813, 75813, 75813, 75813, 75813, 213),
    (207534, 2763015, 1144992, 2883940, 1092932, 661665, 594979, 1150274, 79233, 77862, 77862, 77862, 77862, 77862, 77862, 77862, 77862, 77862, 77862, 126),
    (1145248, 668239, 160896, 330021, 1141765, 1081700, 2175010, 1143812, 71757, 1092867, 2102401, 79911, 79911, 79911, 79911, 79911, 79911, 79911, 79911, 228),
    (721289, 2884142, 1399143, 2243210, 2951553, 143651, 333158, 2627909, 353637, 74754, 82948, 81960, 81960, 81960, 81960, 81960, 81960, 81960, 81960, 247),
    (592010, 350312, 2362696, 131490, 597024, 2889831, 2243586, 598086, 2176388, 2697221, 84009, 84009, 84009, 84009, 84009, 84009, 84009, 84009, 84009, 117),
    (1151403, 1139305, 2247074, 1087587, 198760, 617473, 337027, 605256, 2101344, 601088, 2243716, 2107654, 87078, 86058, 86058, 86058, 86058, 86058, 86058, 125),
    (741548, 1073811, 2249091, 215725, 860258, 2102537, 134179, 83076, 2165157, 2369600, 2163720, 536839, 2178470, 88107, 88107, 88107, 88107, 88107, 88107, 95),
    (860333, 2840651, 619028, 2367909, 2369603, 341027, 2642026, 2896169, 866306, 2166880, 199216, 2113832, 2098177, 2112521, 90156, 90156, 90156, 90156, 90156, 119),
    (356837, 2842700, 1156229, 6566, 2371947, 73895, 869475, 1148039, 2775074, 2900074, 2162688, 19458, 2106378, 2181153, 93185, 92205, 92205, 92205, 92205, 223),
    (209005, 2372143, 867661, 1092999, 344101, 156741, 74888, 806188, 2162816, 613572, 6705, 2300170, 69665, 2233419, 2444330, 95233, 94254, 94254, 94254, 95),
    (344551, 3699054, 1142152, 1082439, 1257865, 3697670, 2424832, 2238565, 74261, 283137, 615585, 89257, 70668, 7435, 2102307, 2106410, 96303, 96303, 96303, 142),
    (887272, 297327, 66568, 870834, 349449, 2118656, 133191, 2309135, 1052718, 71750, 2165862, 2167822, 2103467, 90125, 2189317, 2173963, 74764, 99332, 98352, 55),
    (229810, 347472, 2771114, 67688, 2246026, 751915, 2429570, 24611, 146447, 2103597, 226348, 336897, 2126887, 13323, 2368614, 2172933, 101389, 100401, 100401, 119),
    (3035306, 2721873, 754091, 2906754, 2166819, 91472, 19852, 214019, 2312621, 9288, 79983, 2171917, 76807, 29829, 2192463, 2174982, 102450, 102450, 102450, 91),
    (88434, 877963, 2265123, 218252, 2366474, 270673, 813424, 2786468, 149637, 2197806, 2912296, 2190373, 2245673, 14703, 13327, 2176039, 104499, 104499, 104499, 149),
    (760236, 2792652, 2367524, 757805, 2910251, 273746, 357413, 2912362, 1147217, 78922, 216400, 2110985, 342024, 97585, 2180103, 2128907, 106548, 106548, 106548, 149),
    (486004, 2793750, 273549, 2172974, 155763, 2188686, 341331, 1147186, 2790470, 88103, 96362, 2656689, 2373672, 3167435, 2129929, 2182152, 109711, 108597, 108597, 85),
    (356725, 763477, 78990, 2793648, 2123821, 96423, 1411148, 629895, 2128940, 83283, 168966, 86153, 2656299, 2114634, 2200587, 2130985, 110646, 110646, 110646, 116),
    (569520, 3178607, 632942, 145841, 3189799, 2126991, 18600, 631953, 889992, 2664105, 2320397, 24851, 88618, 2202642, 2120714, 2188342, 112695, 112695, 112695, 68),
    (491705, 82073, 100471, 316424, 2395223, 3307567, 102518, 2273798, 85138, 21070, 108723, 1137673, 92212, 1139754, 2131533, 2192907, 2141708, 2137108, 114744, 51),
    (315512, 2197713, 87128, 2396210, 366711, 18480, 2276368, 369674, 1210411, 2325164, 242222, 2137129, 2382870, 2385486, 2140213, 3172397, 117780, 116793, 116793, 51),
    (299522, 2345049, 231971, 368819, 1395762, 98424, 91224, 21651, 2185355, 2184209, 2130039, 371279, 2122839, 2402349, 2401327, 95245, 2207766, 119822, 118842, 49),
    (250403, 2281651, 368690, 2119723, 370777, 2136108, 2403449, 35916, 3246134, 1140784, 2386040, 2131094, 2278548, 2134190, 2125879, 2275407, 121903, 120891, 120891, 17),
    (252084, 2284036, 370732, 235642, 93333, 2281654, 2405395, 103444, 2123865, 94263, 2397305, 2122766, 34863, 2146360, 2195472, 2198543, 123927, 122940, 122940, 17),
    (254133, 2402821, 373852, 2404397, 2123899, 1060884, 375899, 94330, 114739, 1408052, 2137166, 2145370, 51250, 2147346, 229425, 3177529, 2130961, 124989, 124989, 17),
    (504358, 2287741, 95254, 108727, 376956, 1407028, 2407516, 2408571, 2139157, 117851, 2390138, 105486, 2137113, 1344538, 2132017, 2195474, 128050, 127038, 127038, 17),
    (377079, 1062974, 2409687, 97310, 379510, 3439702, 98333, 240793, 54333, 100973, 2132028, 226512, 300060, 120884, 2462805, 2269747, 2268187, 130106, 129087, 0),
)
EVENTS = 2 * (len(PLAN[0]) - 1)
ROWS = 256
BLOCK = 512
INFO = 16
SLOT = 2 * ROWS + INFO


def pick(values, index):
    result = jnp.int32(values[0])
    for at in range(1, len(values)):
        result = jnp.where(index == at, jnp.int32(values[at]), result)
    return result


def kernel(
    x_hbm, gain_hbm, wqkv_hbm, wout_hbm, seg_hbm, out_ref,
    xbuf, gain_ref, wqkv, wcol, seg_ref, kv, give, qgive, qrows, qmask, acc, run_max, run_sum, ogive, att,
    local_sem, x_send, x_recv, w_send, w_recv, s_send, s_recv, kv_send, kv_recv, o_send, o_recv,
):
    f32, bf16 = jnp.float32, jnp.bfloat16
    seq, head = lax.axis_index("seq"), lax.axis_index("head")
    core = lax.rem(seq, 2)
    chip = lax.div(seq, 2)
    z = lax.rem(chip, 8)
    x = lax.div(chip, 8)
    other = 1 - core

    def at(xx, zz, cc):
        return (xx * 8 + zz) * 2 + cc

    z_up, z_down = lax.rem(z + 1, 8), lax.rem(z + 7, 8)
    x_up, x_down = lax.rem(x + 1, 4), lax.rem(x + 3, 4)
    up = (at(x, z_up, core), head)
    down = (at(x, z_down, core), head)
    right = (at(x_up, z, core), head)
    left = (at(x_down, z, core), head)
    partner = (at(x, z, other), head)
    y_of = [lax.rem(head + j, 4) for j in range(4)]

    barrier = pltpu.get_barrier_semaphore()
    greeted = [up, down, right, left, partner]
    for j in range(1, 4):
        greeted.append((seq, y_of[j]))
        greeted.append((at(x, z, other), y_of[j]))
    for device in greeted:
        pl.semaphore_signal(barrier, inc=1, device_id=device, device_id_type=MESH)

    seg_in = pltpu.make_async_copy(seg_hbm, seg_ref, local_sem.at[3])
    seg_in.start()
    gain_in = pltpu.make_async_copy(gain_hbm, gain_ref, local_sem.at[4])
    gain_in.start()
    mine = pltpu.make_async_copy(x_hbm, xbuf.at[head], local_sem.at[0])
    mine.start()
    weights_in = pltpu.make_async_copy(wqkv_hbm, wqkv, local_sem.at[1])
    weights_in.start()
    columns = pl.ds(pl.multiple_of(head * ROWS, ROWS), ROWS)
    wcol_in = pltpu.make_async_copy(wout_hbm.at[:, columns], wcol.at[head], local_sem.at[2])
    wcol_in.start()

    pl.semaphore_wait(barrier, len(greeted))

    x_copies = []
    for j in (2, 1, 3):
        copy = pltpu.make_async_remote_copy(
            src_ref=x_hbm, dst_ref=xbuf.at[head], send_sem=x_send.at[j], recv_sem=x_recv.at[head],
            device_id=(seq, y_of[j]), device_id_type=MESH)
        copy.start()
        x_copies.append(copy)
    seg_in.wait()
    seg = seg_ref[...]
    lane = lax.broadcasted_iota(jnp.int32, (1, HD), 1)
    sub = lax.broadcasted_iota(jnp.int32, (INFO, HD), 0)
    lower = jnp.zeros((1, HD), f32)
    upper = jnp.zeros((1, HD), f32)
    for t in range(1, 5):
        before = jnp.sum(jnp.where(seg < t, 1.0, 0.0).astype(f32), axis=1, keepdims=True)
        before = before[0:1] + before[1:2]
        lower = jnp.where(lane == t, before, lower)
        upper = jnp.where(lane == t - 1, before, upper)
    lower = jnp.where(lane < 4, lower, 0.0)
    info = jnp.where(sub == 0, lower, jnp.where(sub == 1, upper, 0.0)).astype(bf16)

    mine_at = core * 32 + chip
    words = [pick([row[i] for row in PLAN], mine_at) for i in range(len(PLAN[0]))]
    gain_in.wait()
    mine.wait()
    weights_in.wait()
    wcol_in.wait()
    for j in range(1, 4):
        pltpu.make_async_remote_copy(
            src_ref=x_hbm, dst_ref=xbuf.at[y_of[j]], send_sem=x_send.at[j], recv_sem=x_recv.at[y_of[j]],
            device_id=(seq, y_of[j]), device_id_type=MESH).wait_recv()

    w_copies = []
    for j in range(1, 4):
        theirs = pl.ds(pl.multiple_of(y_of[j] * ROWS, ROWS), ROWS)
        copy = pltpu.make_async_remote_copy(
            src_ref=wout_hbm.at[:, theirs], dst_ref=wcol.at[head], send_sem=w_send.at[j],
            recv_sem=w_recv.at[head], device_id=(seq, y_of[j]), device_id_type=MESH)
        copy.start()
        w_copies.append(copy)

    parts = [xbuf[y].astype(f32) for y in range(4)]
    squares = sum(jnp.sum(part * part, axis=1, keepdims=True) for part in parts)
    scale = lax.rsqrt(squares * (1.0 / 1024.0) + epsilon)
    normed = jnp.concatenate(
        [(parts[y] * scale * gain_ref[:, y * ROWS : (y + 1) * ROWS]).astype(bf16) for y in range(4)], axis=1)

    def project(which):
        return jnp.dot(normed, wqkv[which], preferred_element_type=f32)

    def hand_on(direction, piece):
        device = (up, down, right, left)[direction]
        return pltpu.make_async_remote_copy(
            src_ref=kv.at[piece], dst_ref=kv.at[piece], send_sem=kv_send.at[direction, piece],
            recv_sem=kv_recv.at[piece], device_id=device, device_id_type=MESH)

    own = pl.ds(pl.multiple_of(core * ROWS, ROWS), ROWS)
    own_piece = core * 32 + chip
    other_piece = other * 32 + chip

    def swap(j, source, target, landing):
        return pltpu.make_async_remote_copy(
            src_ref=source, dst_ref=target, send_sem=s_send.at[j], recv_sem=landing,
            device_id=partner, device_id_type=MESH)

    give[2 * ROWS : SLOT, :] = info
    kv[own_piece, 2 * ROWS : SLOT, :] = info
    for j in (1, 2):
        both = project(j).astype(bf16)
        first, second = both[:, :HD], both[:, HD:]
        give[(j - 1) * ROWS : j * ROWS, :] = jnp.where(core == 0, second, first)
        kv[own_piece, (j - 1) * ROWS : j * ROWS, :] = jnp.where(core == 0, first, second)

    own_flag = [lax.rem(lax.div(words[-1], 1 << i), 2) == 1 for i in range(8)]
    s_copies = [swap(0, give, kv.at[own_piece], kv_recv.at[own_piece])]
    s_copies[0].start()
    for direction in range(4):
        @pl.when(own_flag[direction])
        def _(direction=direction):
            hand_on(direction, own_piece).start()

    both = (project(0) * (1.0 / math.sqrt(HD))).astype(bf16)
    first, second = both[:, :HD], both[:, HD:]
    qgive[...] = jnp.where(core == 0, second, first)
    s_copies.append(swap(1, qgive, qrows.at[own], s_recv.at[1]))
    s_copies[1].start()
    qrows[own, :] = jnp.where(core == 0, first, second)

    swap(0, give, kv.at[other_piece], kv_recv.at[other_piece]).wait_recv()
    for direction in range(4):
        @pl.when(own_flag[4 + direction])
        def _(direction=direction):
            hand_on(direction, other_piece).start()
    s_copies[1].wait_recv()

    def event(e):
        pair = lax.div(e, 2)
        word = words[0]
        for i in range(1, len(words) - 1):
            word = jnp.where(pair == i, words[i], word)
        code = jnp.where(lax.rem(e, 2) == 0, lax.rem(word, 2048), lax.div(word, 2048))
        piece = lax.rem(code, 64)
        flag = [lax.rem(lax.div(code, 64 << i), 2) == 1 for i in range(5)]
        source = lax.rem(piece, 32)
        return source != chip, piece, source, flag

    row = lax.broadcasted_iota(jnp.int32, (ROWS, HD), 0).astype(f32)
    lanes = lax.broadcasted_iota(jnp.int32, (ROWS, HD), 1)

    def inside(piece):
        bounds = kv[piece, 2 * ROWS : SLOT, :].astype(f32)
        return (row >= bounds[0:1, :]) & (row < bounds[1:2, :])

    for half in range(2):
        qmask[half * ROWS : (half + 1) * ROWS, :] = jnp.where(
            inside(half * 32 + chip) | (lanes >= 4), 0.0, masked_score).astype(bf16)

    def keys_of(piece):
        return jnp.concatenate(
            [kv[piece, 0:ROWS, :], jnp.where(inside(piece), 1.0, 0.0).astype(bf16)], axis=1)

    def scores_of(part, keys):
        rows = slice(part * ROWS, (part + 1) * ROWS)
        queries = jnp.concatenate([qrows[rows, :], qmask[rows, :]], axis=1)
        return lax.dot_general(queries, keys, (((1,), (1,)), ((), ())), preferred_element_type=f32)

    def keep(part, new_max, total, product):
        rows = slice(part * ROWS, (part + 1) * ROWS)
        run_max[rows, :] = jnp.broadcast_to(new_max, (ROWS, HD))
        run_sum[rows, :] = jnp.broadcast_to(total, (ROWS, HD))
        acc[rows, :] = product

    own_keys = [keys_of(chip), keys_of(32 + chip)]
    own_values = [kv[half * 32 + chip, ROWS : 2 * ROWS, :] for half in range(2)]
    q_at = lax.broadcasted_iota(jnp.int32, (ROWS, ROWS), 0)
    k_at = lax.broadcasted_iota(jnp.int32, (ROWS, ROWS), 1)
    for part in range(2):
        scores = [scores_of(part, own_keys[half]) for half in range(part + 1)]
        scores[part] = jnp.where(k_at <= q_at, scores[part], masked_score)
        new_max = jnp.max(scores[part], axis=1, keepdims=True)
        if part == 1:
            new_max = jnp.maximum(new_max, jnp.max(scores[0], axis=1, keepdims=True))
        total, product = 0.0, 0.0
        for half in range(part + 1):
            weights = jnp.exp(scores[half] - new_max)
            total = total + jnp.sum(weights, axis=1, keepdims=True)
            product = product + jnp.dot(
                weights.astype(bf16), own_values[half], preferred_element_type=f32)
        keep(part, new_max, total, product)

    def attend(source):
        keys = jnp.concatenate([keys_of(source), keys_of(32 + source)], axis=0)
        values = jnp.concatenate(
            [kv[half * 32 + source, ROWS : 2 * ROWS, :] for half in range(2)], axis=0)
        queries = jnp.concatenate([qrows[...], qmask[...]], axis=1)
        scores = lax.dot_general(
            queries, keys, (((1,), (1,)), ((), ())), preferred_element_type=f32)
        old_max = run_max[...]
        new_max = jnp.maximum(old_max, jnp.max(scores, axis=1, keepdims=True))
        weights = jnp.exp(scores - jnp.concatenate([new_max] * (BLOCK // HD), axis=1))
        factor = jnp.exp(old_max - new_max)
        run_max[...] = new_max
        run_sum[...] = run_sum[...] * factor + jnp.sum(weights, axis=1, keepdims=True)
        acc[...] = acc[...] * factor + jnp.dot(
            weights.astype(bf16), values, preferred_element_type=f32)

    def step(e, carry):
        valid, piece, source, flag = event(e)

        @pl.when(valid)
        def _():
            hand_on(0, piece).wait_recv()
            for direction in range(4):
                @pl.when(flag[direction])
                def _(direction=direction):
                    hand_on(direction, piece).start()

            @pl.when(flag[4])
            def _():
                attend(source)

        return carry

    lax.fori_loop(0, EVENTS, step, 0)

    for half in range(2):
        rows = slice(half * ROWS, (half + 1) * ROWS)
        ogive[half] = (acc[rows, :] / run_sum[rows, 0:1]).astype(bf16)

    o_copies = []
    lot = head * 2 + core
    for j in (2, 1, 3, 0):
        for c in range(2):
            if j == 0 and c == 0:
                continue
            row_core = core if c == 0 else other
            copy = pltpu.make_async_remote_copy(
                src_ref=ogive.at[row_core], dst_ref=att.at[lot], send_sem=o_send.at[j * 2 + c],
                recv_sem=o_recv.at[lot], device_id=(at(x, z, row_core), y_of[j]), device_id_type=MESH)
            copy.start()
            o_copies.append(copy)
    att[lot] = ogive[core]

    for direction in range(8):
        @pl.when(own_flag[direction])
        def _(direction=direction):
            hand_on(direction % 4, own_piece if direction < 4 else other_piece).wait_send()

    def drain(e, carry):
        valid, piece, source, flag = event(e)
        for direction in range(4):
            @pl.when(flag[direction])
            def _(direction=direction):
                hand_on(direction, piece).wait_send()
        return carry

    lax.fori_loop(0, EVENTS, drain, 0)
    for copy in x_copies + w_copies + s_copies:
        copy.wait_send()

    for j in range(1, 4):
        pltpu.make_async_remote_copy(
            src_ref=wout_hbm.at[:, columns], dst_ref=wcol.at[y_of[j]], send_sem=w_send.at[j],
            recv_sem=w_recv.at[y_of[j]], device_id=(seq, y_of[j]), device_id_type=MESH).wait_recv()
    total = None
    for j in (0, 1, 3, 2):
        for c in range(2):
            if j == 0 and c == 0:
                continue
            lot_of = y_of[j] * 2 + (core if c == 0 else other)
            pltpu.make_async_remote_copy(
                src_ref=ogive.at[core], dst_ref=att.at[lot_of], send_sem=o_send.at[j * 2 + c],
                recv_sem=o_recv.at[lot_of], device_id=partner, device_id_type=MESH).wait_recv()
        both = jnp.concatenate([att[2 * y_of[j]], att[2 * y_of[j] + 1]], axis=1)
        term = jnp.dot(both, wcol[y_of[j]], preferred_element_type=f32)
        total = term if total is None else total + term
    out_ref[...] = total.astype(bf16)

    for copy in o_copies:
        copy.wait_send()


def per_device(face_rows, norm_gain, w_qkv, w_out, segments):
    bf16, f32 = jnp.bfloat16, jnp.float32
    vmem = pl.BlockSpec(memory_space=pltpu.VMEM)
    hbm = pl.BlockSpec(memory_space=pl.ANY)
    dma = pltpu.SemaphoreType.DMA
    return pl.pallas_call(
        kernel,
        name="face_attention",
        out_shape=jax.ShapeDtypeStruct((ROWS, ROWS), bf16),
        in_specs=[hbm, hbm, hbm, hbm, hbm],
        out_specs=vmem,
        scratch_shapes=[
            pltpu.VMEM((4, ROWS, ROWS), bf16),
            pltpu.VMEM((1, 1024), f32),
            pltpu.VMEM((3, 1024, ROWS), bf16),
            pltpu.VMEM((4, ROWS, ROWS), bf16),
            pltpu.VMEM((2, HD), jnp.int32),
            pltpu.VMEM((64, SLOT, HD), bf16),
            pltpu.VMEM((SLOT, HD), bf16),
            pltpu.VMEM((ROWS, HD), bf16),
            pltpu.VMEM((BLOCK, HD), bf16),
            pltpu.VMEM((BLOCK, HD), bf16),
            pltpu.VMEM((BLOCK, HD), f32),
            pltpu.VMEM((BLOCK, HD), f32),
            pltpu.VMEM((BLOCK, HD), f32),
            pltpu.VMEM((2, ROWS, HD), bf16),
            pltpu.VMEM((8, ROWS, HD), bf16),
            dma((5,)),
            dma((4,)), dma((4,)),
            dma((4,)), dma((4,)),
            dma((4,)), dma((4,)),
            dma((4, 64)), dma((64,)),
            dma((8,)), dma((8,)),
        ],
        compiler_params=pltpu.CompilerParams(
            collective_id=0, has_side_effects=True, vmem_limit_bytes=67043328),
    )(
        face_rows,
        norm_gain.reshape(1, 1024),
        jnp.transpose(w_qkv, (1, 0, 2)),
        w_out,
        segments.reshape(2, HD),
    )


def solution(mesh):
    in_specs = (P("seq", "head"), P(), P(None, None, "head"), P("head", None), P("seq"))
    out_specs = P("seq", "head")
    return jax.shard_map(
        per_device, mesh=mesh, in_specs=in_specs, out_specs=out_specs, check_vma=False
    )
```
